32 devices in a mesh: seq: 16 (over z, y, x), dp: 2 (over core).
Axes of the slice: x: 2, y: 2, z: 4, core: 2. Of those that a mesh axis runs over, the one named last changes fastest.
Arguments:
- glu_input: bfloat16 [2, 12288, 1024], P('dp', 'seq'), may hold values from -2500 to 2500
- out_grad: bfloat16 [2, 12288, 1024], P('dp', 'seq'), may hold values from -50 to 50
- lengths: int32 [2], replicated, may hold values from 6144 to 12288, as said below
- depth_weight: float32 [512, 31], replicated, may hold values from -1.5 to 1.5
- bn_gain: float32 [512], replicated, may hold values from 0.5 to 2
- bn_shift: float32 [512], replicated, may hold values from -1 to 1
- proj_weight: bfloat16 [512, 1024], P('seq', 'dp'), may hold values from -0.25 to 0.25
Outputs:
- input_grad: bfloat16 [2, 12288, 1024], P('dp', 'seq')
- proj_grad: float32 [512, 1024], P('seq', 'dp')
- depth_grad: float32 [512, 31], P('seq')
- gain_grad: float32 [512], P('seq')
- shift_grad: float32 [512], P('seq')
The draws below stay inside these ranges and needn't reach their ends.
Inputs may be any that keep to these rules, and one draw needn't show every extreme that they name: `lengths`: at least one utterance has all 12288 frames valid.
All inputs are finite; a program needn't handle non-finite values.
Results may differ from the reference program's by a relative error of at most 0.0061.
Values may be sent and summed in bfloat16 or wider, within the bound.
A program may use at most 64 MiB of HBM per device.

```python
import math
import jax
import jax.numpy as jnp
from jax import lax

C = 512
D = 1024
KERNEL = 31
HALF = 15
LENGTH = 12288
UTTS = 2


def draw_glu_input(key, part):
    keys = jax.random.split(jax.random.fold_in(key, 17), 5)
    shape = (UTTS, LENGTH, 2 * C)
    frames = jnp.arange(LENGTH, dtype=jnp.float32) / LENGTH
    noise = jnp.clip(jax.random.normal(keys[0], shape, jnp.float32), -4.0, 4.0)
    offsets = jax.random.uniform(keys[1], (2 * C,), jnp.float32, -1.5, 1.5)
    ramp_up = 1.0 + 2.0 * frames
    value_scale = jnp.exp(jax.random.uniform(keys[2], (C,), jnp.float32, 0.0, math.log(10.0)))
    gate_scale = 0.3 * jnp.exp(jax.random.uniform(keys[3], (C,), jnp.float32, 0.0, math.log(2.0)))
    columns = jnp.concatenate([value_scale, gate_scale])
    rough = jnp.exp(jax.random.uniform(keys[4], (UTTS, LENGTH, 1), jnp.float32, 0.0, math.log(4.0)))
    return ((offsets + noise) * columns * rough * ramp_up[None, :, None]).astype(jnp.bfloat16)


def draw_out_grad(key, part):
    keys = jax.random.split(jax.random.fold_in(key, 29), 2)
    shape = (UTTS, LENGTH, D)
    frames = jnp.arange(LENGTH, dtype=jnp.float32) / LENGTH
    rough = jnp.exp(jax.random.uniform(keys[1], (UTTS, LENGTH, 1), jnp.float32, 0.0, math.log(3.0)))
    ramp_up = 1.0 + 2.0 * frames
    noise = jnp.clip(jax.random.normal(keys[0], shape, jnp.float32), -4.0, 4.0)
    return (noise * rough * ramp_up[None, :, None]).astype(jnp.bfloat16)


def draw_lengths(key, part):
    keys = jax.random.split(jax.random.fold_in(key, 41), 2)
    base = jax.random.randint(keys[0], (UTTS,), LENGTH // 2, LENGTH + 1, dtype=jnp.int32)
    chosen = jax.random.randint(keys[1], (), 0, UTTS, dtype=jnp.int32)
    return jnp.where(jnp.arange(UTTS, dtype=jnp.int32) == chosen, jnp.int32(LENGTH), base).astype(jnp.int32)


def steps_of(own_key, shape, shards, smallest, top_value):
    level = 1.0
    for dim, blocks in shards:
        draws = jax.random.uniform(jax.random.fold_in(jax.random.fold_in(own_key, 6), dim), (blocks,), jnp.float32, smallest / len(shards), top_value / len(shards))
        level = level * jnp.repeat(jnp.exp(draws), shape[dim] // blocks).reshape((-1,) + (1,) * (len(shape) - 1 - dim))
    return level


def scatter_about(key, extent, scale, bound, pieces=(), held_as=jnp.bfloat16):
    result = scale * jax.random.normal(key, extent, jnp.float32)
    if pieces:
        result = result * steps_of(key, extent, pieces, -0.22, 0.18)
    return jnp.clip(result, -bound, bound).astype(held_as)


def setup_inputs(seed: int = 0) -> dict:
    key_of = jax.random.split(jax.random.key(seed), 8)
    return {
        "glu_input": draw_glu_input(jax.random.fold_in(key_of[7], 71), 0),
        "out_grad": draw_out_grad(jax.random.fold_in(key_of[7], 71), 0),
        "lengths": draw_lengths(jax.random.fold_in(key_of[7], 71), 0),
        "depth_weight": scatter_about(key_of[3], (C, KERNEL), 0.25, 1.5, (), jnp.float32),
        "bn_gain": jnp.clip(jax.random.uniform(key_of[4], (C,), jnp.float32, 0.5, 2.0), 0.5, 2.0),
        "bn_shift": jnp.clip(jax.random.uniform(key_of[5], (C,), jnp.float32, -1.0, 1.0), -1.0, 1.0),
        "proj_weight": scatter_about(key_of[6], (C, D), C ** -0.5, 0.25, ((0, 16), (1, 2))),
    }


EPSILON = 1e-05

def recompute(glu_row, length, depth_weight):
    frames = jnp.arange(LENGTH, dtype=jnp.int32)
    frame_mask = (frames < length).astype(jnp.float32)[:, None]
    values = glu_row[:, :C].astype(jnp.float32)
    gate_sigmoid = jax.nn.sigmoid(glu_row[:, C:].astype(jnp.float32))
    glu_out = (values * gate_sigmoid * frame_mask).astype(jnp.bfloat16)
    padded = jnp.pad(glu_out, ((HALF, HALF), (0, 0))).astype(jnp.float32)
    conv_out = jnp.zeros((LENGTH, C), jnp.float32)
    for offset in range(KERNEL):
        conv_out = conv_out + depth_weight[:, offset] * padded[offset:offset + LENGTH]
    return (frame_mask, values, gate_sigmoid, padded, conv_out)

def reference(glu_input, out_grad, lengths, depth_weight, bn_gain, bn_shift, proj_weight):
    frame_count = jnp.sum(lengths).astype(jnp.float32)
    grad_scale = float(UTTS * LENGTH) ** (-0.5)

    def conv_sums(utterance):
        frame_mask, _, _, _, conv_out = recompute(utterance[0], utterance[1], depth_weight)
        return lax.optimization_barrier(jnp.sum(frame_mask * conv_out, axis=0))
    mean_val = lax.optimization_barrier(jnp.sum(lax.map(conv_sums, (glu_input, lengths)), axis=0)) / frame_count

    def conv_squares(utterance):
        frame_mask, _, _, _, conv_out = recompute(utterance[0], utterance[1], depth_weight)
        return lax.optimization_barrier(jnp.sum(frame_mask * jnp.square(conv_out - mean_val), axis=0))
    variance = lax.optimization_barrier(jnp.sum(lax.map(conv_squares, (glu_input, lengths)), axis=0)) / frame_count
    inv_std = lax.rsqrt(variance + EPSILON)

    def backward_act(utterance):
        glu_row, grad_row, length = utterance
        frame_mask, values, gate_sigmoid, padded, conv_out = recompute(glu_row, length, depth_weight)
        normed = (conv_out - mean_val) * inv_std
        pre_act = bn_gain * normed + bn_shift
        pre_sig = jax.nn.sigmoid(pre_act)
        act_out = (frame_mask * pre_act * pre_sig).astype(jnp.bfloat16)
        act_grad = frame_mask * jnp.dot(grad_row, proj_weight.T, preferred_element_type=jnp.float32)
        pre_grad = act_grad * pre_sig * (1.0 + pre_act * (1.0 - pre_sig))
        return (frame_mask, values, gate_sigmoid, padded, normed, act_out, pre_grad)

    def second(utterance):
        _, _, _, _, normed, act_out, pre_grad = backward_act(utterance)
        weight_part = jnp.dot(act_out.T, utterance[1], preferred_element_type=jnp.float32)
        return (weight_part, lax.optimization_barrier(jnp.sum(pre_grad * normed, axis=0)), lax.optimization_barrier(jnp.sum(pre_grad, axis=0)))
    weight_parts, gain_parts, shift_parts = lax.map(second, (glu_input, out_grad, lengths))
    proj_grad = grad_scale * lax.optimization_barrier(jnp.sum(weight_parts, axis=0))
    gain_sum = lax.optimization_barrier(jnp.sum(gain_parts, axis=0))
    shift_sum = lax.optimization_barrier(jnp.sum(shift_parts, axis=0))

    def third(utterance):
        frame_mask, values, gate_sigmoid, padded, normed, _, pre_grad = backward_act(utterance)
        conv_grad = (frame_mask * inv_std * bn_gain * (pre_grad - shift_sum / frame_count - normed * gain_sum / frame_count)).astype(jnp.bfloat16)
        conv_wide = conv_grad.astype(jnp.float32)
        depth_part = jnp.stack([lax.optimization_barrier(jnp.sum(conv_wide * padded[offset:offset + LENGTH], axis=0)) for offset in range(KERNEL)], axis=1)
        grad_pad = jnp.pad(conv_wide, ((HALF, HALF), (0, 0)))
        glu_grad = jnp.zeros((LENGTH, C), jnp.float32)
        for offset in range(KERNEL):
            glu_grad = glu_grad + depth_weight[:, offset] * grad_pad[2 * HALF - offset:2 * HALF - offset + LENGTH]
        glu_grad = glu_grad * frame_mask
        input_row = jnp.concatenate([glu_grad * gate_sigmoid, glu_grad * values * gate_sigmoid * (1.0 - gate_sigmoid)], axis=1)
        return (input_row.astype(jnp.bfloat16), depth_part)
    input_grad, depth_parts = lax.map(third, (glu_input, out_grad, lengths))
    depth_grad = grad_scale * lax.optimization_barrier(jnp.sum(depth_parts, axis=0))
    return (input_grad, proj_grad, depth_grad, grad_scale * gain_sum, grad_scale * shift_sum)
```

```python
import functools

import jax
import jax.numpy as jnp
from jax import lax
from jax.experimental import pallas as pl
from jax.experimental.pallas import tpu as pltpu
from jax.sharding import PartitionSpec as P

EPSILON = 1e-05
LANES = 128
EDGE = 16
MESH = pl.DeviceIdType.MESH


class Exchange:
    def __init__(self, axis, count, me, source, target, landed, send, recv):
        self.axis, self.count, self.me = axis, count, me
        self.source, self.target, self.landed = source, target, landed
        self.send, self.recv = send, recv

    def peer(self, step):
        return lax.rem(self.me + step, self.count)

    def start(self):
        def body(step, carry):
            peer = self.peer(step)
            pltpu.make_async_remote_copy(
                self.source(peer), self.target(), self.send.at[peer], self.recv.at[self.me],
                device_id={self.axis: peer}, device_id_type=MESH,
            ).start()
            return carry

        lax.fori_loop(1, self.count, body, 0)

    def wait(self, which):
        def body(step, carry):
            peer = self.peer(step)
            copy = pltpu.make_async_remote_copy(
                self.source(peer), self.landed(peer), self.send.at[peer], self.recv.at[peer],
                device_id={self.axis: peer}, device_id_type=MESH,
            )
            copy.wait_recv() if which == "recv" else copy.wait_send()
            return carry

        lax.fori_loop(1, self.count, body, 0)


def fused(dims, x_hbm, og_hbm, w_hbm, len_ref, taps_ref, gain_ref, shift_ref,
          in_out, proj_out, depth_out, sums_out,
          x, og, sig, pad, conv, act_grad, act, gpad, halo_s, halo_r, ghalo_s, ghalo_r,
          wall, w2, st1d, st1s, st2d, st2s, psend, prd, ps2, prs, dscr, dsend, drs, dd,
          in_sem, hs_sem, hr_sem, gs_sem, gr_sem, wgs, wgr, wds, wdr,
          a1, b1, a2, b2, a3, b3, a4, b4, pds, pdr, pss, psr, dss, dsr, dds, ddr):
    seq_n, dp_n, frames, channels, width, kernel, grad_scale = dims
    half = (kernel - 1) // 2
    blocks = channels // LANES
    rows, cols = channels // seq_n, width // dp_n
    seq, dp = lax.axis_index("seq"), lax.axis_index("dp")
    f32, bf16 = jnp.float32, jnp.bfloat16

    top = pltpu.make_async_copy(x_hbm.at[0, pl.ds(0, EDGE)], x.at[pl.ds(0, EDGE)], in_sem.at[0])
    bottom = pltpu.make_async_copy(
        x_hbm.at[0, pl.ds(frames - EDGE, EDGE)], x.at[pl.ds(frames - EDGE, EDGE)], in_sem.at[1]
    )
    middle = pltpu.make_async_copy(
        x_hbm.at[0, pl.ds(EDGE, frames - 2 * EDGE)],
        x.at[pl.ds(EDGE, frames - 2 * EDGE)], in_sem.at[2],
    )
    own_w = pltpu.make_async_copy(w_hbm, wall.at[dp, seq], in_sem.at[3])
    og_copy = pltpu.make_async_copy(og_hbm.at[0], og, in_sem.at[4])
    for copy in (top, bottom, own_w, middle, og_copy):
        copy.start()

    barrier = pltpu.get_barrier_semaphore()
    for axis, count, me in (("seq", seq_n, seq), ("dp", dp_n, dp)):
        def greet(step, carry):
            pl.semaphore_signal(barrier, inc=1, device_id={axis: lax.rem(me + step, count)},
                                device_id_type=MESH)
            return carry

        lax.fori_loop(1, count, greet, 0)

    length = len_ref[dp]
    total = lax.fori_loop(0, len_ref.shape[0], lambda i, s: s + len_ref[i], jnp.int32(0))
    inv_count = 1.0 / jnp.full((1, LANES), total.astype(f32), f32)
    first = seq * frames

    def mask_of(start, size):
        at = lax.broadcasted_iota(jnp.int32, (size, LANES), 0) + (first + start)
        return jnp.where(at < length, 1.0, 0.0).astype(f32)

    def glu(start, size, block):
        lanes = pl.ds(block * LANES, LANES)
        gates = pl.ds(channels + block * LANES, LANES)
        s = jax.nn.sigmoid(x[pl.ds(start, size), gates].astype(f32))
        sig[block, pl.ds(start, size), :] = s
        out = x[pl.ds(start, size), lanes].astype(f32) * s * mask_of(start, size)
        return out.astype(bf16)

    top.wait()
    bottom.wait()
    own_w.wait()
    for block in range(blocks):
        lanes = pl.ds(block * LANES, LANES)
        low, high = glu(0, EDGE, block), glu(frames - EDGE, EDGE, block)
        halo_s[0, :, lanes] = low
        halo_s[1, :, lanes] = high
        pad[block, pl.ds(EDGE, EDGE), :] = low.astype(f32)
        pad[block, pl.ds(frames, EDGE), :] = high.astype(f32)

    pl.semaphore_wait(barrier, seq_n + dp_n - 2)

    def halo_copy(which, send, recv, ssem, rsem):
        to = seq - 1 if which == 0 else seq + 1
        return pltpu.make_async_remote_copy(
            send.at[which], recv.at[1 - which], ssem.at[which], rsem.at[1 - which],
            device_id={"seq": to}, device_id_type=MESH,
        )

    def halo_start(*args):
        @pl.when(seq > 0)
        def _():
            halo_copy(0, *args).start()

        @pl.when(seq < seq_n - 1)
        def _():
            halo_copy(1, *args).start()

    def halo_wait(send, recv, ssem, rsem, into):
        @pl.when(seq > 0)
        def _():
            halo_copy(1, send, recv, ssem, rsem).wait_recv()
            for block in range(blocks):
                into[block, pl.ds(0, EDGE), :] = recv[0, :, pl.ds(block * LANES, LANES)].astype(f32)

        @pl.when(seq == 0)
        def _():
            for block in range(blocks):
                into[block, pl.ds(0, EDGE), :] = jnp.zeros((EDGE, LANES), f32)

        @pl.when(seq < seq_n - 1)
        def _():
            halo_copy(0, send, recv, ssem, rsem).wait_recv()
            for block in range(blocks):
                into[block, pl.ds(EDGE + frames, EDGE), :] = recv[
                    1, :, pl.ds(block * LANES, LANES)].astype(f32)

        @pl.when(seq == seq_n - 1)
        def _():
            for block in range(blocks):
                into[block, pl.ds(EDGE + frames, EDGE), :] = jnp.zeros((EDGE, LANES), f32)

    def halo_done(*args):
        @pl.when(seq > 0)
        def _():
            halo_copy(0, *args).wait_send()

        @pl.when(seq < seq_n - 1)
        def _():
            halo_copy(1, *args).wait_send()

    glu_halo = (halo_s, halo_r, hs_sem, hr_sem)
    grad_halo = (ghalo_s, ghalo_r, gs_sem, gr_sem)
    halo_start(*glu_halo)

    def exchange(axis, source, target, landed, send, recv):
        count, me = (seq_n, seq) if axis == "seq" else (dp_n, dp)
        return Exchange(axis, count, me, source, target, landed, send, recv)

    w_seq = exchange("seq", lambda p: wall.at[dp, seq], lambda: wall.at[dp, seq],
                     lambda p: wall.at[dp, p], wgs, wgr)
    w_dp = exchange("dp", lambda p: wall.at[dp], lambda: wall.at[dp], lambda p: wall.at[p],
                    wds, wdr)
    w_seq.start()

    middle.wait()
    chunk = 32
    inner = (frames - 2 * EDGE) // chunk

    def glu_body(i, carry):
        start = pl.multiple_of(EDGE + i * chunk, EDGE)
        for block in range(blocks):
            pad[block, pl.ds(EDGE + start, chunk), :] = glu(start, chunk, block).astype(f32)
        return carry

    lax.fori_loop(0, inner, glu_body, 0)
    halo_wait(*glu_halo, pad)

    def fold(v):
        return jnp.sum(v.reshape(v.shape[0] // 8, 8, LANES), axis=0)

    step_rows = 64
    steps = frames // step_rows

    def conv_block(block):
        lanes = pl.ds(block * LANES, LANES)

        def body(i, carry):
            start = pl.multiple_of(i * step_rows, step_rows)
            acc = jnp.zeros((step_rows, LANES), f32)
            for k in range(kernel):
                acc = acc + taps_ref[pl.ds(k, 1), lanes] * pad[
                    block, pl.ds(start + (EDGE - half + k), step_rows), :]
            conv[block, pl.ds(start, step_rows), :] = acc
            masked = acc * mask_of(start, step_rows)
            return carry[0] + fold(masked), carry[1] + fold(masked * acc)

        zero = jnp.zeros((8, LANES), f32)
        s, q = lax.fori_loop(0, steps, body, (zero, zero))
        return jnp.sum(s, axis=0, keepdims=True), jnp.sum(q, axis=0, keepdims=True)

    def reduce_pair(buf_d, buf_s, sems):
        d = exchange("dp", lambda p: buf_d.at[dp], lambda: buf_d.at[dp], lambda p: buf_d.at[p],
                     sems[0], sems[1])
        s = exchange("seq", lambda p: buf_s.at[seq], lambda: buf_s.at[seq], lambda p: buf_s.at[p],
                     sems[2], sems[3])
        return d, s

    def add_up(buf, count):
        return lax.fori_loop(1, count, lambda i, acc: acc + buf[i], buf[0])

    def stack(parts):
        first_half = jnp.concatenate([p[0] for p in parts], axis=0)
        return jnp.concatenate([first_half] + [p[1] for p in parts], axis=0)

    st1_dp, st1_seq = reduce_pair(st1d, st1s, (a1, b1, a2, b2))
    st1d[dp] = stack([conv_block(block) for block in range(blocks)])
    st1_dp.start()
    w_seq.wait("recv")
    w_dp.start()
    st1_dp.wait("recv")
    st1s[seq] = add_up(st1d, dp_n)
    st1_seq.start()

    w_dp.wait("recv")
    for d in range(dp_n):
        w2[:, pl.ds(d * cols, cols)] = wall[d].astype(f32).reshape(channels, cols).astype(bf16)
    og_copy.wait()
    mm_rows = 128

    def act_body(i, carry):
        at = pl.ds(pl.multiple_of(i * mm_rows, mm_rows), mm_rows)
        act_grad[at, :] = lax.dot_general(og[at, :], w2[...], (((1,), (1,)), ((), ())),
                                          preferred_element_type=f32)
        return carry

    lax.fori_loop(0, frames // mm_rows, act_body, 0)

    st1_seq.wait("recv")
    stats = add_up(st1s, seq_n)
    mean = stats[0:blocks] * inv_count
    variance = stats[blocks:] * inv_count - mean * mean
    inv_std = lax.rsqrt(variance + EPSILON)

    def pre_block(block):
        lanes = pl.ds(block * LANES, LANES)
        m, r = mean[block:block + 1], inv_std[block:block + 1]
        g, b = gain_ref[:, lanes], shift_ref[:, lanes]

        def body(i, carry):
            start = pl.multiple_of(i * step_rows, step_rows)
            at = pl.ds(start, step_rows)
            mask = mask_of(start, step_rows)
            normed = (conv[block, at, :] - m) * r
            pre_act = g * normed + b
            s = jax.nn.sigmoid(pre_act)
            act[at, lanes] = (mask * pre_act * s).astype(bf16)
            pre_grad = mask * act_grad[at, lanes] * s * (1.0 + pre_act * (1.0 - s))
            act_grad[at, lanes] = pre_grad
            return carry[0] + fold(pre_grad * normed), carry[1] + fold(pre_grad)

        zero = jnp.zeros((8, LANES), f32)
        s, q = lax.fori_loop(0, steps, body, (zero, zero))
        return jnp.sum(s, axis=0, keepdims=True), jnp.sum(q, axis=0, keepdims=True)

    st2_dp, st2_seq = reduce_pair(st2d, st2s, (a3, b3, a4, b4))
    st2d[dp] = stack([pre_block(block) for block in range(blocks)])
    st2_dp.start()

    per = LANES // rows
    p_dp = exchange("dp", lambda p: psend.at[p], lambda: prd.at[dp], lambda p: prd.at[p], pds, pdr)
    p_seq = exchange("seq", lambda p: ps2.at[p], lambda: prs.at[seq], lambda p: prs.at[p], pss, psr)

    def project(block):
        for d in range(dp_n):
            term = lax.dot_general(
                act[:, pl.ds(block * LANES, LANES)], og[:, pl.ds(d * cols, cols)],
                (((0,), (0,)), ((), ())), preferred_element_type=f32)
            psend[d, pl.ds(block * per, per)] = term.reshape(per, rows, cols).astype(bf16)

    for block in range(blocks // 2):
        project(block)
    st2_dp.wait("recv")
    st2s[seq] = add_up(st2d, dp_n)
    st2_seq.start()
    for block in range(blocks // 2, blocks):
        project(block)
    p_dp.start()

    st2_seq.wait("recv")
    sums = add_up(st2s, seq_n)
    sums_out[...] = sums * grad_scale
    gain_mean, shift_mean = sums[0:blocks] * inv_count, sums[blocks:] * inv_count

    def conv_grad(start, size, block):
        lanes = pl.ds(block * LANES, LANES)
        m, r = mean[block:block + 1], inv_std[block:block + 1]
        at = pl.ds(start, size)
        normed = (conv[block, at, :] - m) * r
        value = mask_of(start, size) * (r * gain_ref[:, lanes]) * (
            act_grad[at, lanes] - shift_mean[block:block + 1] - normed * gain_mean[block:block + 1])
        return value.astype(bf16)

    for block in range(blocks):
        lanes = pl.ds(block * LANES, LANES)
        low, high = conv_grad(0, EDGE, block), conv_grad(frames - EDGE, EDGE, block)
        ghalo_s[0, :, lanes] = low
        ghalo_s[1, :, lanes] = high
        gpad[block, pl.ds(EDGE, EDGE), :] = low.astype(f32)
        gpad[block, pl.ds(frames, EDGE), :] = high.astype(f32)
    halo_start(*grad_halo)

    def grad_body(i, carry):
        start = pl.multiple_of(EDGE + i * chunk, EDGE)
        for block in range(blocks):
            gpad[block, pl.ds(EDGE + start, chunk), :] = conv_grad(start, chunk, block).astype(f32)
        return carry

    lax.fori_loop(0, inner, grad_body, 0)

    p_dp.wait("recv")

    def add_dp(j, carry):
        def term(step, acc):
            return acc + prd[lax.rem(dp + step, dp_n), j].astype(f32)

        ps2[j] = lax.fori_loop(1, dp_n, term, psend[dp, j].astype(f32)).astype(bf16)
        return carry

    lax.fori_loop(0, seq_n, add_dp, 0)
    p_seq.start()

    small = 32
    d_seq = exchange("seq", lambda p: dsend.at[p], lambda: drs.at[seq], lambda p: drs.at[p],
                     dss, dsr)
    d_dp = exchange("dp", lambda p: dd.at[dp], lambda: dd.at[dp], lambda p: dd.at[p], dds, ddr)
    dscr[...] = jnp.zeros_like(dscr)
    for block in range(blocks):
        def depth_body(i, accs):
            start = pl.multiple_of(i * small, small)
            g = gpad[block, pl.ds(EDGE + start, small), :]
            return tuple(
                acc + fold(g * pad[block, pl.ds(start + (EDGE - half + k), small), :])
                for k, acc in enumerate(accs))

        accs = lax.fori_loop(0, frames // small, depth_body,
                             tuple(jnp.zeros((8, LANES), f32) for _ in range(kernel)))
        for k in range(kernel):
            dscr[pl.ds(k, 1), :] = jnp.sum(accs[k], axis=0, keepdims=True)
        dsend[pl.ds(block * per, per)] = jnp.transpose(dscr[...]).reshape(per, rows, LANES)
    d_seq.start()
    halo_wait(*grad_halo, gpad)

    def back_block(block):
        lanes = pl.ds(block * LANES, LANES)
        gates = pl.ds(channels + block * LANES, LANES)

        def body(i, carry):
            start = pl.multiple_of(i * step_rows, step_rows)
            at = pl.ds(start, step_rows)
            acc = jnp.zeros((step_rows, LANES), f32)
            for k in range(kernel):
                acc = acc + taps_ref[pl.ds(k, 1), lanes] * gpad[
                    block, pl.ds(start + (EDGE + half - k), step_rows), :]
            s = sig[block, at, :]
            scaled = acc * mask_of(start, step_rows) * s
            in_out[0, at, lanes] = scaled.astype(bf16)
            in_out[0, at, gates] = (scaled * x[at, lanes].astype(f32) * (1.0 - s)).astype(bf16)
            return carry

        lax.fori_loop(0, steps, body, 0)

    for block in range(blocks // 2):
        back_block(block)
    d_seq.wait("recv")
    dd[dp] = lax.fori_loop(
        1, seq_n, lambda i, acc: acc + drs[lax.rem(seq + i, seq_n)], dsend[seq])
    d_dp.start()
    for block in range(blocks // 2, blocks):
        back_block(block)

    p_seq.wait("recv")
    proj_out[...] = grad_scale * lax.fori_loop(
        1, seq_n, lambda i, acc: acc + prs[lax.rem(seq + i, seq_n)].astype(f32),
        ps2[seq].astype(f32))
    d_dp.wait("recv")
    depth_out[...] = grad_scale * add_up(dd, dp_n)

    halo_done(*glu_halo)
    halo_done(*grad_halo)
    for one in (w_seq, w_dp, st1_dp, st1_seq, st2_dp, st2_seq, p_dp, p_seq, d_seq, d_dp):
        one.wait("send")


def on_device(glu_input, out_grad, lengths, depth_weight, bn_gain, bn_shift, proj_weight):
    utts, frames, doubled = glu_input.shape
    channels, width = doubled // 2, out_grad.shape[2]
    kernel = depth_weight.shape[1]
    seq_n, dp_n = lax.axis_size("seq"), lax.axis_size("dp")
    rows, cols = channels // seq_n, width // dp_n
    blocks = channels // LANES
    assert utts == 1
    grad_scale = float(utts * dp_n * frames * seq_n) ** (-0.5)
    taps = jnp.transpose(depth_weight)
    f32, bf16 = jnp.float32, jnp.bfloat16
    vmem, dma = pltpu.VMEM, pltpu.SemaphoreType.DMA
    dims = (seq_n, dp_n, frames, channels, width, kernel, grad_scale)
    held = pl.BlockSpec(memory_space=pltpu.VMEM)
    apart = pl.BlockSpec(memory_space=pl.ANY)
    padded = frames + 2 * EDGE
    stat = (2 * blocks, LANES)
    input_grad, proj_grad, depth_grad, sums = pl.pallas_call(
        functools.partial(fused, dims),
        out_shape=(
            jax.ShapeDtypeStruct((1, frames, doubled), bf16),
            jax.ShapeDtypeStruct((rows, cols), f32),
            jax.ShapeDtypeStruct((rows, LANES), f32),
            jax.ShapeDtypeStruct(stat, f32),
        ),
        in_specs=[apart, apart, apart, pl.BlockSpec(memory_space=pltpu.SMEM), held, held, held],
        out_specs=(held, held, held, held),
        scratch_shapes=[
            vmem((frames, doubled), bf16),
            vmem((frames, width), bf16),
            vmem((blocks, frames, LANES), f32),
            vmem((blocks, padded, LANES), f32),
            vmem((blocks, frames, LANES), f32),
            vmem((frames, channels), f32),
            vmem((frames, channels), bf16),
            vmem((blocks, padded, LANES), f32),
            vmem((2, EDGE, channels), bf16),
            vmem((2, EDGE, channels), bf16),
            vmem((2, EDGE, channels), bf16),
            vmem((2, EDGE, channels), bf16),
            vmem((dp_n, seq_n, rows, cols), bf16),
            vmem((channels, width), bf16),
            vmem((dp_n,) + stat, f32),
            vmem((seq_n,) + stat, f32),
            vmem((dp_n,) + stat, f32),
            vmem((seq_n,) + stat, f32),
            vmem((dp_n, seq_n, rows, cols), bf16),
            vmem((dp_n, seq_n, rows, cols), bf16),
            vmem((seq_n, rows, cols), bf16),
            vmem((seq_n, rows, cols), bf16),
            vmem((LANES, LANES), f32),
            vmem((seq_n, rows, LANES), f32),
            vmem((seq_n, rows, LANES), f32),
            vmem((dp_n, rows, LANES), f32),
            dma((5,)), dma((2,)), dma((2,)), dma((2,)), dma((2,)),
            dma((seq_n,)), dma((seq_n,)), dma((dp_n,)), dma((dp_n,)),
            dma((dp_n,)), dma((dp_n,)), dma((seq_n,)), dma((seq_n,)),
            dma((dp_n,)), dma((dp_n,)), dma((seq_n,)), dma((seq_n,)),
            dma((dp_n,)), dma((dp_n,)), dma((seq_n,)), dma((seq_n,)),
            dma((seq_n,)), dma((seq_n,)), dma((dp_n,)), dma((dp_n,)),
        ],
        compiler_params=pltpu.CompilerParams(
            collective_id=0, has_side_effects=True, vmem_limit_bytes=56 * 1024 * 1024),
    )(glu_input, out_grad, proj_weight, lengths, taps, bn_gain[None], bn_shift[None])
    start = lax.axis_index("seq") * rows
    gain_grad = lax.dynamic_slice_in_dim(sums[:blocks].reshape(channels), start, rows)
    shift_grad = lax.dynamic_slice_in_dim(sums[blocks:].reshape(channels), start, rows)
    return input_grad, proj_grad, depth_grad[:, :kernel], gain_grad, shift_grad


def solution(mesh):
    return jax.shard_map(
        on_device,
        mesh=mesh,
        in_specs=(P("dp", "seq", None), P("dp", "seq", None), P(), P(), P(), P(), P("seq", "dp")),
        out_specs=(P("dp", "seq", None), P("seq", "dp"), P("seq", None), P("seq"), P("seq")),
        check_vma=False,
    )
```

```python
import functools

import jax
import jax.numpy as jnp
from jax import lax
from jax.experimental import pallas as pl
from jax.experimental.pallas import tpu as pltpu
from jax.sharding import PartitionSpec as P

EPSILON = 1e-05
LANES = 128
EDGE = 16
MESH = pl.DeviceIdType.MESH


class Exchange:
    def __init__(self, to, count, me, source, target, landed, send, recv):
        self.to, self.count, self.me = to, count, me
        self.source, self.target, self.landed = source, target, landed
        self.send, self.recv = send, recv

    def peer(self, step):
        return lax.rem(self.me + step, self.count)

    def start(self):
        def body(step, carry):
            peer = self.peer(step)
            pltpu.make_async_remote_copy(
                self.source(peer), self.target(), self.send.at[peer], self.recv.at[self.me],
                device_id=self.to(peer), device_id_type=MESH,
            ).start()
            return carry

        lax.fori_loop(1, self.count, body, 0)

    def wait(self, which):
        def body(step, carry):
            peer = self.peer(step)
            copy = pltpu.make_async_remote_copy(
                self.source(peer), self.landed(peer), self.send.at[peer], self.recv.at[peer],
                device_id=self.to(peer), device_id_type=MESH,
            )
            copy.wait_recv() if which == "recv" else copy.wait_send()
            return carry

        lax.fori_loop(1, self.count, body, 0)


def fused(dims, x_hbm, og_hbm, w_hbm, len_ref, taps_ref, gain_ref, shift_ref,
          in_out, proj_out, depth_out, sums_out,
          x, og, sig, pad, conv, act_grad, act, gpad, halo_s, halo_r, ghalo_s, ghalo_r,
          wall, w2, st1d, st1s, st2d, st2s, psend, prd, ps2, prl, ps3, prh, dscr, dturn, dd, dh, dhr, dl,
          in_sem, hs_sem, hr_sem, gs_sem, gr_sem, whs, whr, wls, wlr, wds, wdr,
          a1, b1, a2, b2, a3, b3, a4, b4, pds, pdr, pls, plr, phs, phr,
          dds, ddr, dhs_sem, dhr_sem, dls_sem, dlr_sem):
    seq_n, dp_n, frames, channels, width, kernel, grad_scale = dims
    half = (kernel - 1) // 2
    blocks = channels // LANES
    rows, cols = channels // seq_n, width // dp_n
    seq, dp = lax.axis_index("seq"), lax.axis_index("dp")
    high_n, low_n = blocks, seq_n // blocks
    high, low = seq // low_n, lax.rem(seq, low_n)
    f32, bf16 = jnp.float32, jnp.bfloat16

    top = pltpu.make_async_copy(x_hbm.at[0, pl.ds(0, EDGE)], x.at[pl.ds(0, EDGE)], in_sem.at[0])
    bottom = pltpu.make_async_copy(
        x_hbm.at[0, pl.ds(frames - EDGE, EDGE)], x.at[pl.ds(frames - EDGE, EDGE)], in_sem.at[1]
    )
    middle = pltpu.make_async_copy(
        x_hbm.at[0, pl.ds(EDGE, frames - 2 * EDGE)],
        x.at[pl.ds(EDGE, frames - 2 * EDGE)], in_sem.at[2],
    )
    own_w = pltpu.make_async_copy(w_hbm, wall.at[dp, high, low], in_sem.at[3])
    og_copy = pltpu.make_async_copy(og_hbm.at[0], og, in_sem.at[4])
    for copy in (top, bottom, own_w, middle, og_copy):
        copy.start()

    barrier = pltpu.get_barrier_semaphore()
    for axis, count, me in (("seq", seq_n, seq), ("dp", dp_n, dp)):
        def greet(step, carry):
            pl.semaphore_signal(barrier, inc=1, device_id={axis: lax.rem(me + step, count)},
                                device_id_type=MESH)
            return carry

        lax.fori_loop(1, count, greet, 0)

    length = len_ref[dp]
    total = lax.fori_loop(0, len_ref.shape[0], lambda i, s: s + len_ref[i], jnp.int32(0))
    inv_count = 1.0 / jnp.full((1, LANES), total.astype(f32), f32)
    first = seq * frames

    def mask_of(start, size):
        at = lax.broadcasted_iota(jnp.int32, (size, LANES), 0) + (first + start)
        return jnp.where(at < length, 1.0, 0.0).astype(f32)

    def glu(start, size, block):
        lanes = pl.ds(block * LANES, LANES)
        gates = pl.ds(channels + block * LANES, LANES)
        s = jax.nn.sigmoid(x[pl.ds(start, size), gates].astype(f32))
        sig[block, pl.ds(start, size), :] = s
        out = x[pl.ds(start, size), lanes].astype(f32) * s * mask_of(start, size)
        return out.astype(bf16)

    top.wait()
    bottom.wait()
    own_w.wait()
    for block in range(blocks):
        lanes = pl.ds(block * LANES, LANES)
        head, tail = glu(0, EDGE, block), glu(frames - EDGE, EDGE, block)
        halo_s[0, :, lanes] = head
        halo_s[1, :, lanes] = tail
        pad[block, pl.ds(EDGE, EDGE), :] = head.astype(f32)
        pad[block, pl.ds(frames, EDGE), :] = tail.astype(f32)

    pl.semaphore_wait(barrier, seq_n + dp_n - 2)

    def halo_copy(which, send, recv, ssem, rsem):
        to = seq - 1 if which == 0 else seq + 1
        return pltpu.make_async_remote_copy(
            send.at[which], recv.at[1 - which], ssem.at[which], rsem.at[1 - which],
            device_id={"seq": to}, device_id_type=MESH,
        )

    def halo_start(*args):
        @pl.when(seq > 0)
        def _():
            halo_copy(0, *args).start()

        @pl.when(seq < seq_n - 1)
        def _():
            halo_copy(1, *args).start()

    def halo_wait(send, recv, ssem, rsem, into):
        @pl.when(seq > 0)
        def _():
            halo_copy(1, send, recv, ssem, rsem).wait_recv()
            for block in range(blocks):
                into[block, pl.ds(0, EDGE), :] = recv[0, :, pl.ds(block * LANES, LANES)].astype(f32)

        @pl.when(seq == 0)
        def _():
            for block in range(blocks):
                into[block, pl.ds(0, EDGE), :] = jnp.zeros((EDGE, LANES), f32)

        @pl.when(seq < seq_n - 1)
        def _():
            halo_copy(0, send, recv, ssem, rsem).wait_recv()
            for block in range(blocks):
                into[block, pl.ds(EDGE + frames, EDGE), :] = recv[
                    1, :, pl.ds(block * LANES, LANES)].astype(f32)

        @pl.when(seq == seq_n - 1)
        def _():
            for block in range(blocks):
                into[block, pl.ds(EDGE + frames, EDGE), :] = jnp.zeros((EDGE, LANES), f32)

    def halo_done(*args):
        @pl.when(seq > 0)
        def _():
            halo_copy(0, *args).wait_send()

        @pl.when(seq < seq_n - 1)
        def _():
            halo_copy(1, *args).wait_send()

    glu_halo = (halo_s, halo_r, hs_sem, hr_sem)
    grad_halo = (ghalo_s, ghalo_r, gs_sem, gr_sem)
    halo_start(*glu_halo)

    def exchange(axis, source, target, landed, send, recv):
        count, me, to = {
            "seq": (seq_n, seq, lambda p: {"seq": p}),
            "dp": (dp_n, dp, lambda p: {"dp": p}),
            "high": (high_n, high, lambda p: {"seq": p * low_n + low}),
            "low": (low_n, low, lambda p: {"seq": high * low_n + p}),
        }[axis]
        return Exchange(to, count, me, source, target, landed, send, recv)

    w_high = exchange("high", lambda p: wall.at[dp, high, low], lambda: wall.at[dp, high, low],
                      lambda p: wall.at[dp, p, low], whs, whr)
    w_low = exchange("low", lambda p: wall.at[dp, :, low], lambda: wall.at[dp, :, low],
                     lambda p: wall.at[dp, :, p], wls, wlr)
    w_dp = exchange("dp", lambda p: wall.at[dp], lambda: wall.at[dp], lambda p: wall.at[p],
                    wds, wdr)
    w_high.start()

    middle.wait()
    chunk = 32
    inner = (frames - 2 * EDGE) // chunk

    def glu_body(i, carry):
        start = pl.multiple_of(EDGE + i * chunk, EDGE)
        for block in range(blocks):
            pad[block, pl.ds(EDGE + start, chunk), :] = glu(start, chunk, block).astype(f32)
        return carry

    lax.fori_loop(0, inner, glu_body, 0)
    w_high.wait("recv")
    w_low.start()
    halo_wait(*glu_halo, pad)

    def fold(v):
        return jnp.sum(v.reshape(v.shape[0] // 8, 8, LANES), axis=0)

    step_rows = 64
    steps = frames // step_rows

    def conv_block(block):
        lanes = pl.ds(block * LANES, LANES)

        def body(i, carry):
            start = pl.multiple_of(i * step_rows, step_rows)
            acc = jnp.zeros((step_rows, LANES), f32)
            for k in range(kernel):
                acc = acc + taps_ref[pl.ds(k, 1), lanes] * pad[
                    block, pl.ds(start + (EDGE - half + k), step_rows), :]
            conv[block, pl.ds(start, step_rows), :] = acc
            masked = acc * mask_of(start, step_rows)
            return carry[0] + fold(masked), carry[1] + fold(masked * acc)

        zero = jnp.zeros((8, LANES), f32)
        s, q = lax.fori_loop(0, steps, body, (zero, zero))
        return jnp.sum(s, axis=0, keepdims=True), jnp.sum(q, axis=0, keepdims=True)

    def reduce_pair(buf_d, buf_s, sems):
        d = exchange("dp", lambda p: buf_d.at[dp], lambda: buf_d.at[dp], lambda p: buf_d.at[p],
                     sems[0], sems[1])
        s = exchange("seq", lambda p: buf_s.at[seq], lambda: buf_s.at[seq], lambda p: buf_s.at[p],
                     sems[2], sems[3])
        return d, s

    def add_up(buf, count):
        return lax.fori_loop(1, count, lambda i, acc: acc + buf[i], buf[0])

    def stack(parts):
        first_half = jnp.concatenate([p[0] for p in parts], axis=0)
        return jnp.concatenate([first_half] + [p[1] for p in parts], axis=0)

    st1_dp, st1_seq = reduce_pair(st1d, st1s, (a1, b1, a2, b2))
    st1d[dp] = stack([conv_block(block) for block in range(blocks)])
    st1_dp.start()
    w_low.wait("recv")
    w_dp.start()
    st1_dp.wait("recv")
    st1s[seq] = add_up(st1d, dp_n)
    st1_seq.start()

    w_dp.wait("recv")
    for d in range(dp_n):
        w2[:, pl.ds(d * cols, cols)] = wall[d].astype(f32).reshape(channels, cols).astype(bf16)
    og_copy.wait()
    mm_rows = 128

    def act_body(i, carry):
        at = pl.ds(pl.multiple_of(i * mm_rows, mm_rows), mm_rows)
        act_grad[at, :] = lax.dot_general(og[at, :], w2[...], (((1,), (1,)), ((), ())),
                                          preferred_element_type=f32)
        return carry

    lax.fori_loop(0, frames // mm_rows, act_body, 0)

    st1_seq.wait("recv")
    stats = add_up(st1s, seq_n)
    mean = stats[0:blocks] * inv_count
    variance = stats[blocks:] * inv_count - mean * mean
    inv_std = lax.rsqrt(variance + EPSILON)

    def pre_block(block):
        lanes = pl.ds(block * LANES, LANES)
        m, r = mean[block:block + 1], inv_std[block:block + 1]
        g, b = gain_ref[:, lanes], shift_ref[:, lanes]

        def body(i, carry):
            start = pl.multiple_of(i * step_rows, step_rows)
            at = pl.ds(start, step_rows)
            mask = mask_of(start, step_rows)
            normed = (conv[block, at, :] - m) * r
            pre_act = g * normed + b
            s = jax.nn.sigmoid(pre_act)
            act[at, lanes] = (mask * pre_act * s).astype(bf16)
            pre_grad = mask * act_grad[at, lanes] * s * (1.0 + pre_act * (1.0 - s))
            act_grad[at, lanes] = pre_grad
            return carry[0] + fold(pre_grad * normed), carry[1] + fold(pre_grad)

        zero = jnp.zeros((8, LANES), f32)
        s, q = lax.fori_loop(0, steps, body, (zero, zero))
        return jnp.sum(s, axis=0, keepdims=True), jnp.sum(q, axis=0, keepdims=True)

    st2_dp, st2_seq = reduce_pair(st2d, st2s, (a3, b3, a4, b4))
    st2d[dp] = stack([pre_block(block) for block in range(blocks)])
    st2_dp.start()

    per = low_n
    p_dp = exchange("dp", lambda p: psend.at[p], lambda: prd.at[dp], lambda p: prd.at[p], pds, pdr)
    p_low = exchange("low", lambda p: ps2.at[:, p], lambda: prl.at[low], lambda p: prl.at[p],
                     pls, plr)
    p_high = exchange("high", lambda p: ps3.at[p], lambda: prh.at[high], lambda p: prh.at[p],
                      phs, phr)

    def project(block):
        for d in range(dp_n):
            term = lax.dot_general(
                act[:, pl.ds(block * LANES, LANES)], og[:, pl.ds(d * cols, cols)],
                (((0,), (0,)), ((), ())), preferred_element_type=f32)
            psend[d, block] = term.reshape(per, rows, cols).astype(bf16)

    for block in range(blocks // 2):
        project(block)
    st2_dp.wait("recv")
    st2s[seq] = add_up(st2d, dp_n)
    st2_seq.start()
    for block in range(blocks // 2, blocks):
        project(block)
    p_dp.start()

    st2_seq.wait("recv")
    sums = add_up(st2s, seq_n)
    sums_out[...] = sums * grad_scale
    gain_mean, shift_mean = sums[0:blocks] * inv_count, sums[blocks:] * inv_count

    def conv_grad(start, size, block):
        lanes = pl.ds(block * LANES, LANES)
        m, r = mean[block:block + 1], inv_std[block:block + 1]
        at = pl.ds(start, size)
        normed = (conv[block, at, :] - m) * r
        value = mask_of(start, size) * (r * gain_ref[:, lanes]) * (
            act_grad[at, lanes] - shift_mean[block:block + 1] - normed * gain_mean[block:block + 1])
        return value.astype(bf16)

    for block in range(blocks):
        lanes = pl.ds(block * LANES, LANES)
        head, tail = conv_grad(0, EDGE, block), conv_grad(frames - EDGE, EDGE, block)
        ghalo_s[0, :, lanes] = head
        ghalo_s[1, :, lanes] = tail
        gpad[block, pl.ds(EDGE, EDGE), :] = head.astype(f32)
        gpad[block, pl.ds(frames, EDGE), :] = tail.astype(f32)
    halo_start(*grad_halo)

    def grad_body(i, carry):
        start = pl.multiple_of(EDGE + i * chunk, EDGE)
        for block in range(blocks):
            gpad[block, pl.ds(EDGE + start, chunk), :] = conv_grad(start, chunk, block).astype(f32)
        return carry

    lax.fori_loop(0, inner, grad_body, 0)

    p_dp.wait("recv")

    def add_dp(at, carry):
        h, j = at // low_n, lax.rem(at, low_n)

        def term(step, acc):
            return acc + prd[lax.rem(dp + step, dp_n), h, j].astype(f32)

        ps2[h, j] = lax.fori_loop(1, dp_n, term, psend[dp, h, j].astype(f32)).astype(bf16)
        return carry

    lax.fori_loop(0, seq_n, add_dp, 0)
    p_low.start()

    small = 32
    d_dp = exchange("dp", lambda p: dd.at[dp], lambda: dd.at[dp], lambda p: dd.at[p], dds, ddr)
    d_high = exchange("high", lambda p: dh.at[p], lambda: dhr.at[high], lambda p: dhr.at[p],
                      dhs_sem, dhr_sem)
    d_low = exchange("low", lambda p: dl.at[low], lambda: dl.at[low], lambda p: dl.at[p],
                     dls_sem, dlr_sem)
    dscr[...] = jnp.zeros_like(dscr)
    dd[dp] = jnp.zeros(dd.shape[1:], f32)
    for block in range(blocks):
        def depth_body(i, accs):
            start = pl.multiple_of(i * small, small)
            g = gpad[block, pl.ds(EDGE + start, small), :]
            return tuple(
                acc + fold(g * pad[block, pl.ds(start + (EDGE - half + k), small), :])
                for k, acc in enumerate(accs))

        accs = lax.fori_loop(0, frames // small, depth_body,
                             tuple(jnp.zeros((8, LANES), f32) for _ in range(kernel)))
        for k in range(kernel):
            dd[dp, block, pl.ds(k, 1), :] = jnp.sum(accs[k], axis=0, keepdims=True)
    d_dp.start()
    p_low.wait("recv")

    def add_low(h, carry):
        ps3[h] = lax.fori_loop(
            1, low_n, lambda i, acc: acc + prl[lax.rem(low + i, low_n), h].astype(f32),
            ps2[h, low].astype(f32)).astype(bf16)
        return carry

    lax.fori_loop(0, high_n, add_low, 0)
    p_high.start()
    halo_wait(*grad_halo, gpad)

    def back_block(block):
        lanes = pl.ds(block * LANES, LANES)
        gates = pl.ds(channels + block * LANES, LANES)

        def body(i, carry):
            start = pl.multiple_of(i * step_rows, step_rows)
            at = pl.ds(start, step_rows)
            acc = jnp.zeros((step_rows, LANES), f32)
            for k in range(kernel):
                acc = acc + taps_ref[pl.ds(k, 1), lanes] * gpad[
                    block, pl.ds(start + (EDGE + half - k), step_rows), :]
            s = sig[block, at, :]
            scaled = acc * mask_of(start, step_rows) * s
            in_out[0, at, lanes] = scaled.astype(bf16)
            in_out[0, at, gates] = (scaled * x[at, lanes].astype(f32) * (1.0 - s)).astype(bf16)
            return carry

        lax.fori_loop(0, steps, body, 0)

    d_dp.wait("recv")
    dh[...] = add_up(dd, dp_n)
    d_high.start()
    for block in range(blocks // 2):
        back_block(block)
    d_high.wait("recv")
    dl[low] = lax.fori_loop(
        1, high_n, lambda i, acc: acc + dhr[lax.rem(high + i, high_n)], dh[high])
    d_low.start()
    for block in range(blocks // 2, blocks):
        back_block(block)

    p_high.wait("recv")
    proj_out[...] = grad_scale * lax.fori_loop(
        1, high_n, lambda i, acc: acc + prh[lax.rem(high + i, high_n)].astype(f32),
        ps3[high].astype(f32))
    d_low.wait("recv")
    dscr[pl.ds(0, dl.shape[1]), :] = add_up(dl, low_n)
    dturn[...] = jnp.transpose(dscr[...])
    depth_out[...] = grad_scale * dturn[pl.ds(pl.multiple_of(low * rows, rows), rows), :]

    halo_done(*glu_halo)
    halo_done(*grad_halo)
    for one in (w_high, w_low, w_dp, st1_dp, st1_seq, st2_dp, st2_seq, p_dp, p_low, p_high,
                d_dp, d_high, d_low):
        one.wait("send")


def on_device(glu_input, out_grad, lengths, depth_weight, bn_gain, bn_shift, proj_weight):
    utts, frames, doubled = glu_input.shape
    channels, width = doubled // 2, out_grad.shape[2]
    kernel = depth_weight.shape[1]
    seq_n, dp_n = lax.axis_size("seq"), lax.axis_size("dp")
    rows, cols = channels // seq_n, width // dp_n
    blocks = channels // LANES
    assert utts == 1 and seq_n % blocks == 0
    high_n, low_n = blocks, seq_n // blocks
    taps_up = -(-kernel // 8) * 8
    grad_scale = float(utts * dp_n * frames * seq_n) ** (-0.5)
    taps = jnp.transpose(depth_weight)
    f32, bf16 = jnp.float32, jnp.bfloat16
    vmem, dma = pltpu.VMEM, pltpu.SemaphoreType.DMA
    dims = (seq_n, dp_n, frames, channels, width, kernel, grad_scale)
    held = pl.BlockSpec(memory_space=pltpu.VMEM)
    apart = pl.BlockSpec(memory_space=pl.ANY)
    padded = frames + 2 * EDGE
    stat = (2 * blocks, LANES)
    input_grad, proj_grad, depth_grad, sums = pl.pallas_call(
        functools.partial(fused, dims),
        out_shape=(
            jax.ShapeDtypeStruct((1, frames, doubled), bf16),
            jax.ShapeDtypeStruct((rows, cols), f32),
            jax.ShapeDtypeStruct((rows, LANES), f32),
            jax.ShapeDtypeStruct(stat, f32),
        ),
        in_specs=[apart, apart, apart, pl.BlockSpec(memory_space=pltpu.SMEM), held, held, held],
        out_specs=(held, held, held, held),
        scratch_shapes=[
            vmem((frames, doubled), bf16),
            vmem((frames, width), bf16),
            vmem((blocks, frames, LANES), f32),
            vmem((blocks, padded, LANES), f32),
            vmem((blocks, frames, LANES), f32),
            vmem((frames, channels), f32),
            vmem((frames, channels), bf16),
            vmem((blocks, padded, LANES), f32),
            vmem((2, EDGE, channels), bf16),
            vmem((2, EDGE, channels), bf16),
            vmem((2, EDGE, channels), bf16),
            vmem((2, EDGE, channels), bf16),
            vmem((dp_n, high_n, low_n, rows, cols), bf16),
            vmem((channels, width), bf16),
            vmem((dp_n,) + stat, f32),
            vmem((seq_n,) + stat, f32),
            vmem((dp_n,) + stat, f32),
            vmem((seq_n,) + stat, f32),
            vmem((dp_n, high_n, low_n, rows, cols), bf16),
            vmem((dp_n, high_n, low_n, rows, cols), bf16),
            vmem((high_n, low_n, rows, cols), bf16),
            vmem((low_n, high_n, rows, cols), bf16),
            vmem((high_n, rows, cols), bf16),
            vmem((high_n, rows, cols), bf16),
            vmem((LANES, LANES), f32),
            vmem((LANES, LANES), f32),
            vmem((dp_n, blocks, taps_up, LANES), f32),
            vmem((blocks, taps_up, LANES), f32),
            vmem((high_n, taps_up, LANES), f32),
            vmem((low_n, taps_up, LANES), f32),
            dma((5,)), dma((2,)), dma((2,)), dma((2,)), dma((2,)),
            dma((high_n,)), dma((high_n,)), dma((low_n,)), dma((low_n,)), dma((dp_n,)), dma((dp_n,)),
            dma((dp_n,)), dma((dp_n,)), dma((seq_n,)), dma((seq_n,)),
            dma((dp_n,)), dma((dp_n,)), dma((seq_n,)), dma((seq_n,)),
            dma((dp_n,)), dma((dp_n,)), dma((low_n,)), dma((low_n,)), dma((high_n,)), dma((high_n,)),
            dma((dp_n,)), dma((dp_n,)), dma((high_n,)), dma((high_n,)), dma((low_n,)), dma((low_n,)),
        ],
        compiler_params=pltpu.CompilerParams(
            collective_id=0, has_side_effects=True, vmem_limit_bytes=56 * 1024 * 1024),
    )(glu_input, out_grad, proj_weight, lengths, taps, bn_gain[None], bn_shift[None])
    start = lax.axis_index("seq") * rows
    gain_grad = lax.dynamic_slice_in_dim(sums[:blocks].reshape(channels), start, rows)
    shift_grad = lax.dynamic_slice_in_dim(sums[blocks:].reshape(channels), start, rows)
    return input_grad, proj_grad, depth_grad[:, :kernel], gain_grad, shift_grad


def solution(mesh):
    return jax.shard_map(
        on_device,
        mesh=mesh,
        in_specs=(P("dp", "seq", None), P("dp", "seq", None), P(), P(), P(), P(), P("seq", "dp")),
        out_specs=(P("dp", "seq", None), P("seq", "dp"), P("seq", None), P("seq"), P("seq")),
        check_vma=False,
    )
```

```python
import functools

import jax
import jax.numpy as jnp
from jax import lax
from jax.experimental import pallas as pl
from jax.experimental.pallas import tpu as pltpu
from jax.sharding import PartitionSpec as P

EPSILON = 1e-05
LANES = 128
EDGE = 16
MESH = pl.DeviceIdType.MESH


class Exchange:
    def __init__(self, to, count, me, source, target, landed, send, recv):
        self.to, self.count, self.me = to, count, me
        self.source, self.target, self.landed = source, target, landed
        self.send, self.recv = send, recv

    def peer(self, step):
        return lax.rem(self.me + step, self.count)

    def start(self):
        def body(step, carry):
            peer = self.peer(step)
            pltpu.make_async_remote_copy(
                self.source(peer), self.target(), self.send.at[peer], self.recv.at[self.me],
                device_id=self.to(peer), device_id_type=MESH,
            ).start()
            return carry

        lax.fori_loop(1, self.count, body, 0)

    def wait(self, which):
        def body(step, carry):
            peer = self.peer(step)
            copy = pltpu.make_async_remote_copy(
                self.source(peer), self.landed(peer), self.send.at[peer], self.recv.at[peer],
                device_id=self.to(peer), device_id_type=MESH,
            )
            copy.wait_recv() if which == "recv" else copy.wait_send()
            return carry

        lax.fori_loop(1, self.count, body, 0)


def fused(dims, x_hbm, og_hbm, w_hbm, len_ref, taps_ref, gain_ref, shift_ref,
          in_out, proj_out, depth_out, gain_out, bias_out,
          x, og, sig, pad, conv, act_grad, act, gpad, halo_s, halo_r, ghalo_s, ghalo_r,
          wall, w2, st1d, st1s, st2d, st2s, psend, prd, ps2, prl, ps3, prh, dscr, dturn, dd, dh, dhr, dl, sums_ref,
          in_sem, hs_sem, hr_sem, gs_sem, gr_sem, whs, whr, wls, wlr, wds, wdr,
          a1, b1, a2, b2, a3, b3, a4, b4, pds, pdr, pls, plr, phs, phr,
          dds, ddr, dhs_sem, dhr_sem, dls_sem, dlr_sem):
    seq_n, dp_n, frames, channels, width, kernel, grad_scale = dims
    half = (kernel - 1) // 2
    blocks = channels // LANES
    rows, cols = channels // seq_n, width // dp_n
    seq, dp = lax.axis_index("seq"), lax.axis_index("dp")
    high_n, low_n = blocks, seq_n // blocks
    high, low = seq // low_n, lax.rem(seq, low_n)
    f32, bf16 = jnp.float32, jnp.bfloat16

    top = pltpu.make_async_copy(x_hbm.at[0, pl.ds(0, EDGE)], x.at[pl.ds(0, EDGE)], in_sem.at[0])
    bottom = pltpu.make_async_copy(
        x_hbm.at[0, pl.ds(frames - EDGE, EDGE)], x.at[pl.ds(frames - EDGE, EDGE)], in_sem.at[1]
    )
    middle = pltpu.make_async_copy(
        x_hbm.at[0, pl.ds(EDGE, frames - 2 * EDGE)],
        x.at[pl.ds(EDGE, frames - 2 * EDGE)], in_sem.at[2],
    )
    own_w = pltpu.make_async_copy(w_hbm, wall.at[dp, high, low], in_sem.at[3])
    og_copy = pltpu.make_async_copy(og_hbm.at[0], og, in_sem.at[4])
    for copy in (top, bottom, own_w, middle, og_copy):
        copy.start()

    barrier = pltpu.get_barrier_semaphore()
    for axis, count, me in (("seq", seq_n, seq), ("dp", dp_n, dp)):
        def greet(step, carry):
            pl.semaphore_signal(barrier, inc=1, device_id={axis: lax.rem(me + step, count)},
                                device_id_type=MESH)
            return carry

        lax.fori_loop(1, count, greet, 0)

    length = len_ref[dp]
    total = lax.fori_loop(0, len_ref.shape[0], lambda i, s: s + len_ref[i], jnp.int32(0))
    inv_count = 1.0 / jnp.full((1, LANES), total.astype(f32), f32)
    first = seq * frames

    def mask_of(start, size):
        at = lax.broadcasted_iota(jnp.int32, (size, LANES), 0) + (first + start)
        return jnp.where(at < length, 1.0, 0.0).astype(f32)

    def glu(start, size, block):
        lanes = pl.ds(block * LANES, LANES)
        gates = pl.ds(channels + block * LANES, LANES)
        s = jax.nn.sigmoid(x[pl.ds(start, size), gates].astype(f32))
        sig[block, pl.ds(start, size), :] = s
        out = x[pl.ds(start, size), lanes].astype(f32) * s * mask_of(start, size)
        return out.astype(bf16)

    top.wait()
    bottom.wait()
    own_w.wait()
    for block in range(blocks):
        lanes = pl.ds(block * LANES, LANES)
        head, tail = glu(0, EDGE, block), glu(frames - EDGE, EDGE, block)
        halo_s[0, :, lanes] = head
        halo_s[1, :, lanes] = tail
        pad[block, pl.ds(EDGE, EDGE), :] = head.astype(f32)
        pad[block, pl.ds(frames, EDGE), :] = tail.astype(f32)

    pl.semaphore_wait(barrier, seq_n + dp_n - 2)

    def halo_copy(which, send, recv, ssem, rsem):
        to = seq - 1 if which == 0 else seq + 1
        return pltpu.make_async_remote_copy(
            send.at[which], recv.at[1 - which], ssem.at[which], rsem.at[1 - which],
            device_id={"seq": to}, device_id_type=MESH,
        )

    def halo_start(*args):
        @pl.when(seq > 0)
        def _():
            halo_copy(0, *args).start()

        @pl.when(seq < seq_n - 1)
        def _():
            halo_copy(1, *args).start()

    def halo_wait(send, recv, ssem, rsem, into):
        @pl.when(seq > 0)
        def _():
            halo_copy(1, send, recv, ssem, rsem).wait_recv()
            for block in range(blocks):
                into[block, pl.ds(0, EDGE), :] = recv[0, :, pl.ds(block * LANES, LANES)].astype(f32)

        @pl.when(seq == 0)
        def _():
            for block in range(blocks):
                into[block, pl.ds(0, EDGE), :] = jnp.zeros((EDGE, LANES), f32)

        @pl.when(seq < seq_n - 1)
        def _():
            halo_copy(0, send, recv, ssem, rsem).wait_recv()
            for block in range(blocks):
                into[block, pl.ds(EDGE + frames, EDGE), :] = recv[
                    1, :, pl.ds(block * LANES, LANES)].astype(f32)

        @pl.when(seq == seq_n - 1)
        def _():
            for block in range(blocks):
                into[block, pl.ds(EDGE + frames, EDGE), :] = jnp.zeros((EDGE, LANES), f32)

    def halo_done(*args):
        @pl.when(seq > 0)
        def _():
            halo_copy(0, *args).wait_send()

        @pl.when(seq < seq_n - 1)
        def _():
            halo_copy(1, *args).wait_send()

    glu_halo = (halo_s, halo_r, hs_sem, hr_sem)
    grad_halo = (ghalo_s, ghalo_r, gs_sem, gr_sem)
    halo_start(*glu_halo)

    def exchange(axis, source, target, landed, send, recv):
        count, me, to = {
            "seq": (seq_n, seq, lambda p: {"seq": p}),
            "dp": (dp_n, dp, lambda p: {"dp": p}),
            "high": (high_n, high, lambda p: {"seq": p * low_n + low}),
            "low": (low_n, low, lambda p: {"seq": high * low_n + p}),
        }[axis]
        return Exchange(to, count, me, source, target, landed, send, recv)

    w_high = exchange("high", lambda p: wall.at[dp, high, low], lambda: wall.at[dp, high, low],
                      lambda p: wall.at[dp, p, low], whs, whr)
    w_low = exchange("low", lambda p: wall.at[dp, :, low], lambda: wall.at[dp, :, low],
                     lambda p: wall.at[dp, :, p], wls, wlr)
    w_dp = exchange("dp", lambda p: wall.at[dp], lambda: wall.at[dp], lambda p: wall.at[p],
                    wds, wdr)
    w_high.start()

    middle.wait()
    chunk = 32
    inner = (frames - 2 * EDGE) // chunk

    def glu_body(i, carry):
        start = pl.multiple_of(EDGE + i * chunk, EDGE)
        for block in range(blocks):
            pad[block, pl.ds(EDGE + start, chunk), :] = glu(start, chunk, block).astype(f32)
        return carry

    lax.fori_loop(0, inner, glu_body, 0)
    w_high.wait("recv")
    w_low.start()
    halo_wait(*glu_halo, pad)

    def fold(v):
        return jnp.sum(v.reshape(v.shape[0] // 8, 8, LANES), axis=0)

    step_rows = 64
    steps = frames // step_rows

    def conv_block(block):
        lanes = pl.ds(block * LANES, LANES)

        def body(i, carry):
            start = pl.multiple_of(i * step_rows, step_rows)
            acc = jnp.zeros((step_rows, LANES), f32)
            for k in range(kernel):
                acc = acc + taps_ref[pl.ds(k, 1), lanes] * pad[
                    block, pl.ds(start + (EDGE - half + k), step_rows), :]
            conv[block, pl.ds(start, step_rows), :] = acc
            masked = acc * mask_of(start, step_rows)
            return carry[0] + fold(masked), carry[1] + fold(masked * acc)

        zero = jnp.zeros((8, LANES), f32)
        s, q = lax.fori_loop(0, steps, body, (zero, zero))
        return jnp.sum(s, axis=0, keepdims=True), jnp.sum(q, axis=0, keepdims=True)

    def reduce_pair(buf_d, buf_s, sems):
        d = exchange("dp", lambda p: buf_d.at[dp], lambda: buf_d.at[dp], lambda p: buf_d.at[p],
                     sems[0], sems[1])
        s = exchange("seq", lambda p: buf_s.at[seq], lambda: buf_s.at[seq], lambda p: buf_s.at[p],
                     sems[2], sems[3])
        return d, s

    def add_up(buf, count):
        return lax.fori_loop(1, count, lambda i, acc: acc + buf[i], buf[0])

    def stack(parts):
        first_half = jnp.concatenate([p[0] for p in parts], axis=0)
        return jnp.concatenate([first_half] + [p[1] for p in parts], axis=0)

    st1_dp, st1_seq = reduce_pair(st1d, st1s, (a1, b1, a2, b2))
    st1d[dp] = stack([conv_block(block) for block in range(blocks)])
    st1_dp.start()
    w_low.wait("recv")
    w_dp.start()
    st1_dp.wait("recv")
    st1s[seq] = add_up(st1d, dp_n)
    st1_seq.start()

    w_dp.wait("recv")
    for d in range(dp_n):
        w2[:, pl.ds(d * cols, cols)] = wall[d].astype(f32).reshape(channels, cols).astype(bf16)
    og_copy.wait()
    mm_rows = 128

    def act_body(i, carry):
        at = pl.ds(pl.multiple_of(i * mm_rows, mm_rows), mm_rows)
        act_grad[at, :] = lax.dot_general(og[at, :], w2[...], (((1,), (1,)), ((), ())),
                                          preferred_element_type=f32)
        return carry

    lax.fori_loop(0, frames // mm_rows, act_body, 0)

    st1_seq.wait("recv")
    stats = add_up(st1s, seq_n)
    mean = stats[0:blocks] * inv_count
    variance = stats[blocks:] * inv_count - mean * mean
    inv_std = lax.rsqrt(variance + EPSILON)

    def pre_block(block):
        lanes = pl.ds(block * LANES, LANES)
        m, r = mean[block:block + 1], inv_std[block:block + 1]
        g, b = gain_ref[:, lanes], shift_ref[:, lanes]

        def body(i, carry):
            start = pl.multiple_of(i * step_rows, step_rows)
            at = pl.ds(start, step_rows)
            mask = mask_of(start, step_rows)
            normed = (conv[block, at, :] - m) * r
            pre_act = g * normed + b
            s = jax.nn.sigmoid(pre_act)
            act[at, lanes] = (mask * pre_act * s).astype(bf16)
            pre_grad = mask * act_grad[at, lanes] * s * (1.0 + pre_act * (1.0 - s))
            act_grad[at, lanes] = pre_grad
            return carry[0] + fold(pre_grad * normed), carry[1] + fold(pre_grad)

        zero = jnp.zeros((8, LANES), f32)
        s, q = lax.fori_loop(0, steps, body, (zero, zero))
        return jnp.sum(s, axis=0, keepdims=True), jnp.sum(q, axis=0, keepdims=True)

    st2_dp, st2_seq = reduce_pair(st2d, st2s, (a3, b3, a4, b4))
    st2d[dp] = stack([pre_block(block) for block in range(blocks)])
    st2_dp.start()

    per = low_n
    p_dp = exchange("dp", lambda p: psend.at[p], lambda: prd.at[dp], lambda p: prd.at[p], pds, pdr)
    p_low = exchange("low", lambda p: ps2.at[:, p], lambda: prl.at[low], lambda p: prl.at[p],
                     pls, plr)
    p_high = exchange("high", lambda p: ps3.at[p], lambda: prh.at[high], lambda p: prh.at[p],
                      phs, phr)

    def project(block):
        for d in range(dp_n):
            term = lax.dot_general(
                act[:, pl.ds(block * LANES, LANES)], og[:, pl.ds(d * cols, cols)],
                (((0,), (0,)), ((), ())), preferred_element_type=f32)
            psend[d, block] = term.reshape(per, rows, cols).astype(bf16)

    for block in range(blocks // 2):
        project(block)
    st2_dp.wait("recv")
    st2s[seq] = add_up(st2d, dp_n)
    st2_seq.start()
    for block in range(blocks // 2, blocks):
        project(block)
    p_dp.start()

    st2_seq.wait("recv")
    sums = add_up(st2s, seq_n)
    sums_ref[...] = sums * grad_scale

    def own(row):
        turned = pltpu.roll(jnp.broadcast_to(sums_ref[pl.ds(row, 1), :], (8, LANES)),
                            lax.rem(LANES - low * rows, LANES), 1)
        return turned[0:1, 0:rows]

    gain_out[...] = own(high)
    bias_out[...] = own(blocks + high)
    gain_mean, shift_mean = sums[0:blocks] * inv_count, sums[blocks:] * inv_count

    def conv_grad(start, size, block):
        lanes = pl.ds(block * LANES, LANES)
        m, r = mean[block:block + 1], inv_std[block:block + 1]
        at = pl.ds(start, size)
        normed = (conv[block, at, :] - m) * r
        value = mask_of(start, size) * (r * gain_ref[:, lanes]) * (
            act_grad[at, lanes] - shift_mean[block:block + 1] - normed * gain_mean[block:block + 1])
        return value.astype(bf16)

    for block in range(blocks):
        lanes = pl.ds(block * LANES, LANES)
        head, tail = conv_grad(0, EDGE, block), conv_grad(frames - EDGE, EDGE, block)
        ghalo_s[0, :, lanes] = head
        ghalo_s[1, :, lanes] = tail
        gpad[block, pl.ds(EDGE, EDGE), :] = head.astype(f32)
        gpad[block, pl.ds(frames, EDGE), :] = tail.astype(f32)
    halo_start(*grad_halo)

    def grad_body(i, carry):
        start = pl.multiple_of(EDGE + i * chunk, EDGE)
        for block in range(blocks):
            gpad[block, pl.ds(EDGE + start, chunk), :] = conv_grad(start, chunk, block).astype(f32)
        return carry

    lax.fori_loop(0, inner, grad_body, 0)

    p_dp.wait("recv")

    def add_dp(at, carry):
        h, j = at // low_n, lax.rem(at, low_n)

        def term(step, acc):
            return acc + prd[lax.rem(dp + step, dp_n), h, j].astype(f32)

        ps2[h, j] = lax.fori_loop(1, dp_n, term, psend[dp, h, j].astype(f32)).astype(bf16)
        return carry

    lax.fori_loop(0, seq_n, add_dp, 0)
    p_low.start()

    small = 32
    d_dp = exchange("dp", lambda p: dd.at[dp], lambda: dd.at[dp], lambda p: dd.at[p], dds, ddr)
    d_high = exchange("high", lambda p: dh.at[p], lambda: dhr.at[high], lambda p: dhr.at[p],
                      dhs_sem, dhr_sem)
    d_low = exchange("low", lambda p: dl.at[low], lambda: dl.at[low], lambda p: dl.at[p],
                     dls_sem, dlr_sem)
    dscr[...] = jnp.zeros_like(dscr)
    dd[dp] = jnp.zeros(dd.shape[1:], f32)
    for block in range(blocks):
        def depth_body(i, accs):
            start = pl.multiple_of(i * small, small)
            g = gpad[block, pl.ds(EDGE + start, small), :]
            return tuple(
                acc + fold(g * pad[block, pl.ds(start + (EDGE - half + k), small), :])
                for k, acc in enumerate(accs))

        accs = lax.fori_loop(0, frames // small, depth_body,
                             tuple(jnp.zeros((8, LANES), f32) for _ in range(kernel)))
        for k in range(kernel):
            dd[dp, block, pl.ds(k, 1), :] = jnp.sum(accs[k], axis=0, keepdims=True)
    d_dp.start()
    p_low.wait("recv")

    def add_low(h, carry):
        ps3[h] = lax.fori_loop(
            1, low_n, lambda i, acc: acc + prl[lax.rem(low + i, low_n), h].astype(f32),
            ps2[h, low].astype(f32)).astype(bf16)
        return carry

    lax.fori_loop(0, high_n, add_low, 0)
    p_high.start()
    halo_wait(*grad_halo, gpad)

    def back_block(block):
        lanes = pl.ds(block * LANES, LANES)
        gates = pl.ds(channels + block * LANES, LANES)

        def body(i, carry):
            start = pl.multiple_of(i * step_rows, step_rows)
            at = pl.ds(start, step_rows)
            acc = jnp.zeros((step_rows, LANES), f32)
            for k in range(kernel):
                acc = acc + taps_ref[pl.ds(k, 1), lanes] * gpad[
                    block, pl.ds(start + (EDGE + half - k), step_rows), :]
            s = sig[block, at, :]
            scaled = acc * mask_of(start, step_rows) * s
            in_out[0, at, lanes] = scaled.astype(bf16)
            in_out[0, at, gates] = (scaled * x[at, lanes].astype(f32) * (1.0 - s)).astype(bf16)
            return carry

        lax.fori_loop(0, steps, body, 0)

    d_dp.wait("recv")
    dh[...] = add_up(dd, dp_n)
    d_high.start()
    for block in range(blocks // 2):
        back_block(block)
    d_high.wait("recv")
    dl[low] = lax.fori_loop(
        1, high_n, lambda i, acc: acc + dhr[lax.rem(high + i, high_n)], dh[high])
    d_low.start()
    for block in range(blocks // 2, blocks):
        back_block(block)

    p_high.wait("recv")
    proj_out[...] = grad_scale * lax.fori_loop(
        1, high_n, lambda i, acc: acc + prh[lax.rem(high + i, high_n)].astype(f32),
        ps3[high].astype(f32))
    d_low.wait("recv")
    dscr[pl.ds(0, dl.shape[1]), :] = add_up(dl, low_n)
    dturn[...] = jnp.transpose(dscr[...])
    depth_out[...] = (grad_scale * dturn[pl.ds(pl.multiple_of(low * rows, rows), rows), :])[:, :kernel]

    halo_done(*glu_halo)
    halo_done(*grad_halo)
    for one in (w_high, w_low, w_dp, st1_dp, st1_seq, st2_dp, st2_seq, p_dp, p_low, p_high,
                d_dp, d_high, d_low):
        one.wait("send")


def put_out(*refs):
    sem = refs[-1]
    count = (len(refs) - 1) // 2
    copies = [pltpu.make_async_copy(refs[i], refs[count + i], sem.at[i]) for i in range(count)]
    for copy in copies:
        copy.start()
    for copy in copies:
        copy.wait()


def on_device(glu_input, out_grad, lengths, depth_weight, bn_gain, bn_shift, proj_weight):
    utts, frames, doubled = glu_input.shape
    channels, width = doubled // 2, out_grad.shape[2]
    kernel = depth_weight.shape[1]
    seq_n, dp_n = lax.axis_size("seq"), lax.axis_size("dp")
    rows, cols = channels // seq_n, width // dp_n
    blocks = channels // LANES
    assert utts == 1 and seq_n % blocks == 0
    high_n, low_n = blocks, seq_n // blocks
    taps_up = -(-kernel // 8) * 8
    grad_scale = float(utts * dp_n * frames * seq_n) ** (-0.5)
    taps = jnp.transpose(depth_weight)
    f32, bf16 = jnp.float32, jnp.bfloat16
    vmem, dma = pltpu.VMEM, pltpu.SemaphoreType.DMA
    dims = (seq_n, dp_n, frames, channels, width, kernel, grad_scale)
    held = pl.BlockSpec(memory_space=pltpu.VMEM)
    apart = pl.BlockSpec(memory_space=pl.ANY)
    padded = frames + 2 * EDGE
    stat = (2 * blocks, LANES)
    shapes = (((1, frames, doubled), bf16), ((rows, cols), f32), ((rows, kernel), f32),
              ((1, rows), f32), ((1, rows), f32))
    results = pl.pallas_call(
        functools.partial(fused, dims),
        out_shape=tuple(pltpu.VMEM(shape, dtype) for shape, dtype in shapes),
        in_specs=[apart, apart, apart, pl.BlockSpec(memory_space=pltpu.SMEM), held, held, held],
        out_specs=(held,) * len(shapes),
        scratch_shapes=[
            vmem((frames, doubled), bf16),
            vmem((frames, width), bf16),
            vmem((blocks, frames, LANES), f32),
            vmem((blocks, padded, LANES), f32),
            vmem((blocks, frames, LANES), f32),
            vmem((frames, channels), f32),
            vmem((frames, channels), bf16),
            vmem((blocks, padded, LANES), f32),
            vmem((2, EDGE, channels), bf16),
            vmem((2, EDGE, channels), bf16),
            vmem((2, EDGE, channels), bf16),
            vmem((2, EDGE, channels), bf16),
            vmem((dp_n, high_n, low_n, rows, cols), bf16),
            vmem((channels, width), bf16),
            vmem((dp_n,) + stat, f32),
            vmem((seq_n,) + stat, f32),
            vmem((dp_n,) + stat, f32),
            vmem((seq_n,) + stat, f32),
            vmem((dp_n, high_n, low_n, rows, cols), bf16),
            vmem((dp_n, high_n, low_n, rows, cols), bf16),
            vmem((high_n, low_n, rows, cols), bf16),
            vmem((low_n, high_n, rows, cols), bf16),
            vmem((high_n, rows, cols), bf16),
            vmem((high_n, rows, cols), bf16),
            vmem((LANES, LANES), f32),
            vmem((LANES, LANES), f32),
            vmem((dp_n, blocks, taps_up, LANES), f32),
            vmem((blocks, taps_up, LANES), f32),
            vmem((high_n, taps_up, LANES), f32),
            vmem((low_n, taps_up, LANES), f32),
            vmem(stat, f32),
            dma((5,)), dma((2,)), dma((2,)), dma((2,)), dma((2,)),
            dma((high_n,)), dma((high_n,)), dma((low_n,)), dma((low_n,)), dma((dp_n,)), dma((dp_n,)),
            dma((dp_n,)), dma((dp_n,)), dma((seq_n,)), dma((seq_n,)),
            dma((dp_n,)), dma((dp_n,)), dma((seq_n,)), dma((seq_n,)),
            dma((dp_n,)), dma((dp_n,)), dma((low_n,)), dma((low_n,)), dma((high_n,)), dma((high_n,)),
            dma((dp_n,)), dma((dp_n,)), dma((high_n,)), dma((high_n,)), dma((low_n,)), dma((low_n,)),
        ],
        compiler_params=pltpu.CompilerParams(
            collective_id=0, has_side_effects=True, vmem_limit_bytes=56 * 1024 * 1024),
    )(glu_input, out_grad, proj_weight, lengths, taps, bn_gain[None], bn_shift[None])
    input_grad, proj_grad, depth_grad, gain_grad, shift_grad = pl.pallas_call(
        put_out,
        out_shape=tuple(jax.ShapeDtypeStruct(shape, dtype) for shape, dtype in shapes),
        in_specs=[held] * len(shapes),
        out_specs=(apart,) * len(shapes),
        scratch_shapes=[dma((len(shapes),))],
    )(*(pltpu.with_memory_space_constraint(r, pltpu.VMEM) for r in results))
    return input_grad, proj_grad, depth_grad, gain_grad[0], shift_grad[0]


def solution(mesh):
    return jax.shard_map(
        on_device,
        mesh=mesh,
        in_specs=(P("dp", "seq", None), P("dp", "seq", None), P(), P(), P(), P(), P("seq", "dp")),
        out_specs=(P("dp", "seq", None), P("seq", "dp"), P("seq", None), P("seq"), P("seq")),
        check_vma=False,
    )
```

```python
import functools

import jax
import jax.numpy as jnp
from jax import lax
from jax.experimental import pallas as pl
from jax.experimental.pallas import tpu as pltpu
from jax.sharding import PartitionSpec as P

EPSILON = 1e-05
LANES = 128
EDGE = 16
MESH = pl.DeviceIdType.MESH


class Exchange:
    def __init__(self, to, count, me, source, target, landed, send, recv):
        self.to, self.count, self.me = to, count, me
        self.source, self.target, self.landed = source, target, landed
        self.send, self.recv = send, recv

    def peer(self, step):
        return lax.rem(self.me + step, self.count)

    def start(self):
        def body(step, carry):
            peer = self.peer(step)
            pltpu.make_async_remote_copy(
                self.source(peer), self.target(), self.send.at[peer], self.recv.at[self.me],
                device_id=self.to(peer), device_id_type=MESH,
            ).start()
            return carry

        lax.fori_loop(1, self.count, body, 0)

    def wait(self, which):
        def body(step, carry):
            peer = self.peer(step)
            copy = pltpu.make_async_remote_copy(
                self.source(peer), self.landed(peer), self.send.at[peer], self.recv.at[peer],
                device_id=self.to(peer), device_id_type=MESH,
            )
            copy.wait_recv() if which == "recv" else copy.wait_send()
            return carry

        lax.fori_loop(1, self.count, body, 0)


def fused(dims, x_hbm, og_hbm, w_hbm, len_ref, taps_ref, gain_ref, shift_ref,
          in_out, proj_out, depth_out, gain_out, bias_out,
          x, og, sig, pad, conv, act_grad, act, gpad, halo_s, halo_r, ghalo_s, ghalo_r,
          wall, w2, st1d, st1s, st2d, st2s, psend, prd, ps2, prl, ps3, prh, dscr, dturn, dd, dh, dhr, dl, sums_ref, lead, odd, trail, mixed,
          in_sem, hs_sem, hr_sem, gs_sem, gr_sem, whs, whr, wls, wlr, wds, wdr,
          a1, b1, a2, b2, a3, b3, a4, b4, pds, pdr, pls, plr, phs, phr,
          dds, ddr, dhs_sem, dhr_sem, dls_sem, dlr_sem):
    seq_n, dp_n, frames, channels, width, kernel, grad_scale = dims
    half = (kernel - 1) // 2
    blocks = channels // LANES
    rows, cols = channels // seq_n, width // dp_n
    seq, dp = lax.axis_index("seq"), lax.axis_index("dp")
    high_n, low_n = blocks, seq_n // blocks
    high, low = seq // low_n, lax.rem(seq, low_n)
    f32, bf16 = jnp.float32, jnp.bfloat16

    top = pltpu.make_async_copy(x_hbm.at[0, pl.ds(0, EDGE)], x.at[pl.ds(0, EDGE)], in_sem.at[0])
    bottom = pltpu.make_async_copy(
        x_hbm.at[0, pl.ds(frames - EDGE, EDGE)], x.at[pl.ds(frames - EDGE, EDGE)], in_sem.at[1]
    )
    middle = pltpu.make_async_copy(
        x_hbm.at[0, pl.ds(EDGE, frames - 2 * EDGE)],
        x.at[pl.ds(EDGE, frames - 2 * EDGE)], in_sem.at[2],
    )
    own_w = pltpu.make_async_copy(w_hbm, wall.at[dp, high, low], in_sem.at[3])
    og_copy = pltpu.make_async_copy(og_hbm.at[0], og, in_sem.at[4])
    for copy in (top, bottom, own_w, middle, og_copy):
        copy.start()

    barrier = pltpu.get_barrier_semaphore()
    for axis, count, me in (("seq", seq_n, seq), ("dp", dp_n, dp)):
        def greet(step, carry):
            pl.semaphore_signal(barrier, inc=1, device_id={axis: lax.rem(me + step, count)},
                                device_id_type=MESH)
            return carry

        lax.fori_loop(1, count, greet, 0)

    length = len_ref[dp]
    total = lax.fori_loop(0, len_ref.shape[0], lambda i, s: s + len_ref[i], jnp.int32(0))
    inv_count = 1.0 / jnp.full((1, LANES), total.astype(f32), f32)
    first = seq * frames

    def mask_of(start, size):
        at = lax.broadcasted_iota(jnp.int32, (size, LANES), 0) + (first + start)
        return jnp.where(at < length, 1.0, 0.0).astype(f32)

    def glu(start, size, block):
        lanes = pl.ds(block * LANES, LANES)
        gates = pl.ds(channels + block * LANES, LANES)
        s = jax.nn.sigmoid(x[pl.ds(start, size), gates].astype(f32))
        sig[block, pl.ds(start, size), :] = s
        out = x[pl.ds(start, size), lanes].astype(f32) * s * mask_of(start, size)
        return out.astype(bf16)

    def exchange(axis, source, target, landed, send, recv):
        count, me, to = {
            "seq": (seq_n, seq, lambda p: {"seq": p}),
            "dp": (dp_n, dp, lambda p: {"dp": p}),
            "high": (high_n, high, lambda p: {"seq": p * low_n + low}),
            "low": (low_n, low, lambda p: {"seq": high * low_n + p}),
        }[axis]
        return Exchange(to, count, me, source, target, landed, send, recv)

    w_high = exchange("high", lambda p: wall.at[dp, high, low], lambda: wall.at[dp, high, low],
                      lambda p: wall.at[dp, p, low], whs, whr)
    w_low = exchange("low", lambda p: wall.at[dp, :, low], lambda: wall.at[dp, :, low],
                     lambda p: wall.at[dp, :, p], wls, wlr)
    w_dp = exchange("dp", lambda p: wall.at[dp], lambda: wall.at[dp], lambda p: wall.at[p],
                    wds, wdr)

    own_w.wait()
    pl.semaphore_wait(barrier, seq_n + dp_n - 2)

    w_high.start()
    top.wait()
    bottom.wait()
    for block in range(blocks):
        lanes = pl.ds(block * LANES, LANES)
        head, tail = glu(0, EDGE, block), glu(frames - EDGE, EDGE, block)
        halo_s[0, :, lanes] = head
        halo_s[1, :, lanes] = tail
        pad[block, pl.ds(EDGE, EDGE), :] = head.astype(f32)
        pad[block, pl.ds(frames, EDGE), :] = tail.astype(f32)

    def halo_copy(which, send, recv, ssem, rsem):
        to = seq - 1 if which == 0 else seq + 1
        return pltpu.make_async_remote_copy(
            send.at[which], recv.at[1 - which], ssem.at[which], rsem.at[1 - which],
            device_id={"seq": to}, device_id_type=MESH,
        )

    def halo_start(*args):
        @pl.when(seq > 0)
        def _():
            halo_copy(0, *args).start()

        @pl.when(seq < seq_n - 1)
        def _():
            halo_copy(1, *args).start()

    def halo_wait(send, recv, ssem, rsem, into):
        @pl.when(seq > 0)
        def _():
            halo_copy(1, send, recv, ssem, rsem).wait_recv()
            for block in range(blocks):
                into[block, pl.ds(0, EDGE), :] = recv[0, :, pl.ds(block * LANES, LANES)].astype(f32)

        @pl.when(seq == 0)
        def _():
            for block in range(blocks):
                into[block, pl.ds(0, EDGE), :] = jnp.zeros((EDGE, LANES), f32)

        @pl.when(seq < seq_n - 1)
        def _():
            halo_copy(0, send, recv, ssem, rsem).wait_recv()
            for block in range(blocks):
                into[block, pl.ds(EDGE + frames, EDGE), :] = recv[
                    1, :, pl.ds(block * LANES, LANES)].astype(f32)

        @pl.when(seq == seq_n - 1)
        def _():
            for block in range(blocks):
                into[block, pl.ds(EDGE + frames, EDGE), :] = jnp.zeros((EDGE, LANES), f32)

    def halo_done(*args):
        @pl.when(seq > 0)
        def _():
            halo_copy(0, *args).wait_send()

        @pl.when(seq < seq_n - 1)
        def _():
            halo_copy(1, *args).wait_send()

    glu_halo = (halo_s, halo_r, hs_sem, hr_sem)
    grad_halo = (ghalo_s, ghalo_r, gs_sem, gr_sem)
    halo_start(*glu_halo)

    middle.wait()
    chunk = 32
    inner = (frames - 2 * EDGE) // chunk

    def glu_body(i, carry):
        start = pl.multiple_of(EDGE + i * chunk, EDGE)
        for block in range(blocks):
            pad[block, pl.ds(EDGE + start, chunk), :] = glu(start, chunk, block).astype(f32)
        return carry

    lax.fori_loop(0, inner // 2, glu_body, 0)
    w_high.wait("recv")
    w_low.start()
    lax.fori_loop(inner // 2, inner, glu_body, 0)
    halo_wait(*glu_halo, pad)

    def fold(v):
        return jnp.sum(v.reshape(v.shape[0] // 8, 8, LANES), axis=0)

    step_rows = 64
    steps = frames // step_rows
    pairs = step_rows // 2
    split_rows = (frames + 2 * EDGE) // 2 // 10
    assert EDGE == half + 1 and kernel % 2 == 1

    def split(src):
        def body(i, carry):
            for block in range(blocks):
                start = i * (2 * split_rows)
                e = src[block, pl.ds(start, split_rows, stride=2), :]
                o = src[block, pl.ds(start + 1, split_rows, stride=2), :]
                later = src[block, pl.ds(start + 2, split_rows, stride=2), :]
                at = pl.ds(pl.multiple_of(i * split_rows, 8), split_rows)
                lead[block, at, :] = e - o
                odd[block, at, :] = o
                trail[block, at, :] = later - o
            return carry

        lax.fori_loop(0, 10, body, 0)

    def mix(tap):
        mixed[pl.ds(0, 1), :] = taps_ref[pl.ds(tap(1), 1), :]
        for n in range(1, (kernel + 1) // 2):
            mixed[pl.ds(n, 1), :] = (
                taps_ref[pl.ds(tap(2 * n), 1), :] + taps_ref[pl.ds(tap(2 * n + 1), 1), :])

    def filtered(block, i, tap):
        lanes = pl.ds(block * LANES, LANES)
        start = pl.multiple_of(i * pairs, pairs)
        zero = jnp.zeros((pairs, LANES), f32)
        one, two, three = zero, zero, zero
        for n in range((kernel + 1) // 2):
            at = pl.ds(start + n, pairs)
            if n:
                one = one + taps_ref[pl.ds(tap(2 * n), 1), lanes] * lead[block, at, :]
            two = two + mixed[pl.ds(n, 1), lanes] * odd[block, at, :]
            three = three + taps_ref[pl.ds(tap(2 * n + 1), 1), lanes] * trail[block, at, :]
        first_row = i * step_rows
        even, later = one + two, two + three
        conv[block, pl.ds(first_row, pairs, stride=2), :] = even
        conv[block, pl.ds(first_row + 1, pairs, stride=2), :] = later
        return even, later

    def forward(j):
        return j - 1

    def backward(j):
        return kernel - j

    mix(forward)
    split(pad)

    def conv_block(block):
        lanes = pl.ds(block * LANES, LANES)

        def body(i, carry):
            even, later = filtered(block, i, forward)
            at = 2 * lax.broadcasted_iota(jnp.int32, (pairs, LANES), 0) + (
                first + i * step_rows)
            m_even = jnp.where(at < length, even, 0.0)
            m_later = jnp.where(at + 1 < length, later, 0.0)
            return (carry[0] + fold(m_even + m_later),
                    carry[1] + fold(m_even * m_even + m_later * m_later))

        zero = jnp.zeros((8, LANES), f32)
        s, q = lax.fori_loop(0, steps, body, (zero, zero))
        return jnp.sum(s, axis=0, keepdims=True), jnp.sum(q, axis=0, keepdims=True)

    def reduce_pair(buf_d, buf_s, sems):
        d = exchange("dp", lambda p: buf_d.at[dp], lambda: buf_d.at[dp], lambda p: buf_d.at[p],
                     sems[0], sems[1])
        s = exchange("seq", lambda p: buf_s.at[seq], lambda: buf_s.at[seq], lambda p: buf_s.at[p],
                     sems[2], sems[3])
        return d, s

    def add_up(buf, count):
        return lax.fori_loop(1, count, lambda i, acc: acc + buf[i], buf[0])

    def stack(parts):
        first_half = jnp.concatenate([p[0] for p in parts], axis=0)
        return jnp.concatenate([first_half] + [p[1] for p in parts], axis=0)

    st1_dp, st1_seq = reduce_pair(st1d, st1s, (a1, b1, a2, b2))
    st1d[dp] = stack([conv_block(block) for block in range(blocks)])
    st1_dp.start()
    w_low.wait("recv")
    w_dp.start()
    st1_dp.wait("recv")
    st1s[seq] = add_up(st1d, dp_n)
    st1_seq.start()

    w_dp.wait("recv")
    for d in range(dp_n):
        w2[:, pl.ds(d * cols, cols)] = wall[d].astype(f32).reshape(channels, cols).astype(bf16)
    og_copy.wait()
    mm_rows = 128

    def act_body(i, carry):
        at = pl.ds(pl.multiple_of(i * mm_rows, mm_rows), mm_rows)
        act_grad[at, :] = lax.dot_general(og[at, :], w2[...], (((1,), (1,)), ((), ())),
                                          preferred_element_type=f32)
        return carry

    lax.fori_loop(0, frames // mm_rows, act_body, 0)

    st1_seq.wait("recv")
    stats = add_up(st1s, seq_n)
    mean = stats[0:blocks] * inv_count
    variance = stats[blocks:] * inv_count - mean * mean
    inv_std = lax.rsqrt(variance + EPSILON)

    def pre_block(block):
        lanes = pl.ds(block * LANES, LANES)
        m, r = mean[block:block + 1], inv_std[block:block + 1]
        g, b = gain_ref[:, lanes], shift_ref[:, lanes]

        def body(i, carry):
            start = pl.multiple_of(i * step_rows, step_rows)
            at = pl.ds(start, step_rows)
            mask = mask_of(start, step_rows)
            normed = (conv[block, at, :] - m) * r
            pre_act = g * normed + b
            s = jax.nn.sigmoid(pre_act)
            act[at, lanes] = (mask * pre_act * s).astype(bf16)
            pre_grad = mask * act_grad[at, lanes] * s * (1.0 + pre_act * (1.0 - s))
            act_grad[at, lanes] = pre_grad
            return carry[0] + fold(pre_grad * normed), carry[1] + fold(pre_grad)

        zero = jnp.zeros((8, LANES), f32)
        s, q = lax.fori_loop(0, steps, body, (zero, zero))
        return jnp.sum(s, axis=0, keepdims=True), jnp.sum(q, axis=0, keepdims=True)

    st2_dp, st2_seq = reduce_pair(st2d, st2s, (a3, b3, a4, b4))
    st2d[dp] = stack([pre_block(block) for block in range(blocks)])
    st2_dp.start()

    per = low_n
    p_dp = exchange("dp", lambda p: psend.at[p], lambda: prd.at[dp], lambda p: prd.at[p], pds, pdr)
    p_low = exchange("low", lambda p: ps2.at[:, p], lambda: prl.at[low], lambda p: prl.at[p],
                     pls, plr)
    p_high = exchange("high", lambda p: ps3.at[p], lambda: prh.at[high], lambda p: prh.at[p],
                      phs, phr)

    def project(block):
        for d in range(dp_n):
            term = lax.dot_general(
                act[:, pl.ds(block * LANES, LANES)], og[:, pl.ds(d * cols, cols)],
                (((0,), (0,)), ((), ())), preferred_element_type=f32)
            psend[d, block] = term.reshape(per, rows, cols).astype(bf16)

    for block in range(blocks // 2):
        project(block)
    st2_dp.wait("recv")
    st2s[seq] = add_up(st2d, dp_n)
    st2_seq.start()
    for block in range(blocks // 2, blocks):
        project(block)
    p_dp.start()

    p_dp.wait("recv")

    def add_dp(at, carry):
        h, j = at // low_n, lax.rem(at, low_n)

        def term(step, acc):
            return acc + prd[lax.rem(dp + step, dp_n), h, j].astype(f32)

        ps2[h, j] = lax.fori_loop(1, dp_n, term, psend[dp, h, j].astype(f32)).astype(bf16)
        return carry

    lax.fori_loop(0, seq_n, add_dp, 0)
    p_low.start()

    st2_seq.wait("recv")
    sums = add_up(st2s, seq_n)
    sums_ref[...] = sums * grad_scale

    def own(row):
        turned = pltpu.roll(jnp.broadcast_to(sums_ref[pl.ds(row, 1), :], (8, LANES)),
                            lax.rem(LANES - low * rows, LANES), 1)
        return turned[0:1, 0:rows]

    gain_out[...] = own(high)
    bias_out[...] = own(blocks + high)
    gain_mean, shift_mean = sums[0:blocks] * inv_count, sums[blocks:] * inv_count

    def conv_grad(start, size, block):
        lanes = pl.ds(block * LANES, LANES)
        m, r = mean[block:block + 1], inv_std[block:block + 1]
        at = pl.ds(start, size)
        normed = (conv[block, at, :] - m) * r
        value = mask_of(start, size) * (r * gain_ref[:, lanes]) * (
            act_grad[at, lanes] - shift_mean[block:block + 1] - normed * gain_mean[block:block + 1])
        return value.astype(bf16)

    for block in range(blocks):
        lanes = pl.ds(block * LANES, LANES)
        head, tail = conv_grad(0, EDGE, block), conv_grad(frames - EDGE, EDGE, block)
        ghalo_s[0, :, lanes] = head
        ghalo_s[1, :, lanes] = tail
        gpad[block, pl.ds(EDGE, EDGE), :] = head.astype(f32)
        gpad[block, pl.ds(frames, EDGE), :] = tail.astype(f32)
    halo_start(*grad_halo)

    def grad_body(i, carry):
        start = pl.multiple_of(EDGE + i * chunk, EDGE)
        for block in range(blocks):
            gpad[block, pl.ds(EDGE + start, chunk), :] = conv_grad(start, chunk, block).astype(f32)
        return carry

    lax.fori_loop(0, inner, grad_body, 0)

    small = 32
    d_dp = exchange("dp", lambda p: dd.at[dp], lambda: dd.at[dp], lambda p: dd.at[p], dds, ddr)
    d_high = exchange("high", lambda p: dh.at[p], lambda: dhr.at[high], lambda p: dhr.at[p],
                      dhs_sem, dhr_sem)
    d_low = exchange("low", lambda p: dl.at[low], lambda: dl.at[low], lambda p: dl.at[p],
                     dls_sem, dlr_sem)
    dscr[...] = jnp.zeros_like(dscr)
    dd[dp] = jnp.zeros(dd.shape[1:], f32)
    for block in range(blocks):
        def depth_body(i, accs):
            start = pl.multiple_of(i * small, small)
            g = gpad[block, pl.ds(EDGE + start, small), :]
            return tuple(
                acc + fold(g * pad[block, pl.ds(start + (EDGE - half + k), small), :])
                for k, acc in enumerate(accs))

        accs = lax.fori_loop(0, frames // small, depth_body,
                             tuple(jnp.zeros((8, LANES), f32) for _ in range(kernel)))
        for k in range(kernel):
            dd[dp, block, pl.ds(k, 1), :] = jnp.sum(accs[k], axis=0, keepdims=True)
    d_dp.start()
    p_low.wait("recv")

    def add_low(h, carry):
        ps3[h] = lax.fori_loop(
            1, low_n, lambda i, acc: acc + prl[lax.rem(low + i, low_n), h].astype(f32),
            ps2[h, low].astype(f32)).astype(bf16)
        return carry

    lax.fori_loop(0, high_n, add_low, 0)
    p_high.start()
    halo_wait(*grad_halo, gpad)
    mix(backward)
    split(gpad)

    def back_block(block):
        lanes = pl.ds(block * LANES, LANES)
        gates = pl.ds(channels + block * LANES, LANES)

        def body(i, carry):
            start = pl.multiple_of(i * step_rows, step_rows)
            at = pl.ds(start, step_rows)
            filtered(block, i, backward)
            acc = conv[block, at, :]
            s = sig[block, at, :]
            scaled = acc * mask_of(start, step_rows) * s
            in_out[0, at, lanes] = scaled.astype(bf16)
            in_out[0, at, gates] = (scaled * x[at, lanes].astype(f32) * (1.0 - s)).astype(bf16)
            return carry

        lax.fori_loop(0, steps, body, 0)

    d_dp.wait("recv")
    dh[...] = add_up(dd, dp_n)
    d_high.start()
    for block in range(blocks // 2):
        back_block(block)
    d_high.wait("recv")
    dl[low] = lax.fori_loop(
        1, high_n, lambda i, acc: acc + dhr[lax.rem(high + i, high_n)], dh[high])
    d_low.start()
    for block in range(blocks // 2, blocks):
        back_block(block)

    p_high.wait("recv")
    proj_out[...] = grad_scale * lax.fori_loop(
        1, high_n, lambda i, acc: acc + prh[lax.rem(high + i, high_n)].astype(f32),
        ps3[high].astype(f32))
    d_low.wait("recv")
    dscr[pl.ds(0, dl.shape[1]), :] = add_up(dl, low_n)
    dturn[...] = jnp.transpose(dscr[...])
    depth_out[...] = (grad_scale * dturn[pl.ds(pl.multiple_of(low * rows, rows), rows), :])[:, :kernel]

    halo_done(*glu_halo)
    halo_done(*grad_halo)
    for one in (w_high, w_low, w_dp, st1_dp, st1_seq, st2_dp, st2_seq, p_dp, p_low, p_high,
                d_dp, d_high, d_low):
        one.wait("send")


def put_out(*refs):
    sem = refs[-1]
    count = (len(refs) - 1) // 2
    copies = [pltpu.make_async_copy(refs[i], refs[count + i], sem.at[i]) for i in range(count)]
    for copy in copies:
        copy.start()
    for copy in copies:
        copy.wait()


def on_device(glu_input, out_grad, lengths, depth_weight, bn_gain, bn_shift, proj_weight):
    utts, frames, doubled = glu_input.shape
    channels, width = doubled // 2, out_grad.shape[2]
    kernel = depth_weight.shape[1]
    seq_n, dp_n = lax.axis_size("seq"), lax.axis_size("dp")
    rows, cols = channels // seq_n, width // dp_n
    blocks = channels // LANES
    assert utts == 1 and seq_n % blocks == 0
    high_n, low_n = blocks, seq_n // blocks
    taps_up = -(-kernel // 8) * 8
    grad_scale = float(utts * dp_n * frames * seq_n) ** (-0.5)
    taps = jnp.transpose(depth_weight)
    f32, bf16 = jnp.float32, jnp.bfloat16
    vmem, dma = pltpu.VMEM, pltpu.SemaphoreType.DMA
    dims = (seq_n, dp_n, frames, channels, width, kernel, grad_scale)
    held = pl.BlockSpec(memory_space=pltpu.VMEM)
    apart = pl.BlockSpec(memory_space=pl.ANY)
    padded = frames + 2 * EDGE
    stat = (2 * blocks, LANES)
    shapes = (((1, frames, doubled), bf16), ((rows, cols), f32), ((rows, kernel), f32),
              ((1, rows), f32), ((1, rows), f32))
    results = pl.pallas_call(
        functools.partial(fused, dims),
        out_shape=tuple(pltpu.VMEM(shape, dtype) for shape, dtype in shapes),
        in_specs=[apart, apart, apart, pl.BlockSpec(memory_space=pltpu.SMEM), held, held, held],
        out_specs=(held,) * len(shapes),
        scratch_shapes=[
            vmem((frames, doubled), bf16),
            vmem((frames, width), bf16),
            vmem((blocks, frames, LANES), f32),
            vmem((blocks, padded + 8, LANES), f32),
            vmem((blocks, frames, LANES), f32),
            vmem((frames, channels), f32),
            vmem((frames, channels), bf16),
            vmem((blocks, padded + 8, LANES), f32),
            vmem((2, EDGE, channels), bf16),
            vmem((2, EDGE, channels), bf16),
            vmem((2, EDGE, channels), bf16),
            vmem((2, EDGE, channels), bf16),
            vmem((dp_n, high_n, low_n, rows, cols), bf16),
            vmem((channels, width), bf16),
            vmem((dp_n,) + stat, f32),
            vmem((seq_n,) + stat, f32),
            vmem((dp_n,) + stat, f32),
            vmem((seq_n,) + stat, f32),
            vmem((dp_n, high_n, low_n, rows, cols), bf16),
            vmem((dp_n, high_n, low_n, rows, cols), bf16),
            vmem((high_n, low_n, rows, cols), bf16),
            vmem((low_n, high_n, rows, cols), bf16),
            vmem((high_n, rows, cols), bf16),
            vmem((high_n, rows, cols), bf16),
            vmem((LANES, LANES), f32),
            vmem((LANES, LANES), f32),
            vmem((dp_n, blocks, taps_up, LANES), f32),
            vmem((blocks, taps_up, LANES), f32),
            vmem((high_n, taps_up, LANES), f32),
            vmem((low_n, taps_up, LANES), f32),
            vmem(stat, f32),
            vmem((blocks, padded // 2, LANES), f32),
            vmem((blocks, padded // 2, LANES), f32),
            vmem((blocks, padded // 2, LANES), f32),
            vmem(((kernel + 1) // 2, channels), f32),
            dma((5,)), dma((2,)), dma((2,)), dma((2,)), dma((2,)),
            dma((high_n,)), dma((high_n,)), dma((low_n,)), dma((low_n,)), dma((dp_n,)), dma((dp_n,)),
            dma((dp_n,)), dma((dp_n,)), dma((seq_n,)), dma((seq_n,)),
            dma((dp_n,)), dma((dp_n,)), dma((seq_n,)), dma((seq_n,)),
            dma((dp_n,)), dma((dp_n,)), dma((low_n,)), dma((low_n,)), dma((high_n,)), dma((high_n,)),
            dma((dp_n,)), dma((dp_n,)), dma((high_n,)), dma((high_n,)), dma((low_n,)), dma((low_n,)),
        ],
        compiler_params=pltpu.CompilerParams(
            collective_id=0, has_side_effects=True, vmem_limit_bytes=56 * 1024 * 1024),
    )(glu_input, out_grad, proj_weight, lengths, taps, bn_gain[None], bn_shift[None])
    input_grad, proj_grad, depth_grad, gain_grad, shift_grad = pl.pallas_call(
        put_out,
        out_shape=tuple(jax.ShapeDtypeStruct(shape, dtype) for shape, dtype in shapes),
        in_specs=[held] * len(shapes),
        out_specs=(apart,) * len(shapes),
        scratch_shapes=[dma((len(shapes),))],
    )(*(pltpu.with_memory_space_constraint(r, pltpu.VMEM) for r in results))
    return input_grad, proj_grad, depth_grad, gain_grad[0], shift_grad[0]


def solution(mesh):
    return jax.shard_map(
        on_device,
        mesh=mesh,
        in_specs=(P("dp", "seq", None), P("dp", "seq", None), P(), P(), P(), P(), P("seq", "dp")),
        out_specs=(P("dp", "seq", None), P("seq", "dp"), P("seq", None), P("seq"), P("seq")),
        check_vma=False,
    )
```
